512 devices in a mesh: batch: 32 (over z_lo, y, core), gy: 4 (over z_hi), gx: 4 (over x).
Axes of the slice: x: 4, y: 8, z: 8 (z_hi: 4, z_lo: 2; z = z_hi * 2 + z_lo), core: 2. Of those that a mesh axis runs over, the one named last changes fastest.
Arguments:
- x_fine: bfloat16 [32, 32, 128, 256], P('batch', 'gy', 'gx'), may hold values from -6 to 6
- dy_fine: bfloat16 [32, 32, 128, 256], P('batch', 'gy', 'gx'), may hold values from -6 to 6
- x_coarse: bfloat16 [32, 16, 16, 1024], P('batch', 'gy', 'gx'), may hold values from -6 to 6
- dy_coarse: bfloat16 [32, 16, 16, 1024], P('batch', 'gy', 'gx'), may hold values from -6 to 6
- timestep: int32 [32], P('batch'), may hold values from 0 to 999
- fine_gain: float32 [256], replicated, may hold values from 0.5 to 2.5, as said below
- coarse_gain: float32 [1024], replicated, may hold values from 0.5 to 2.5, as said below
- fine_qkv: bfloat16 [256, 768], replicated, may hold values from -0.375 to 0.375
- fine_out: bfloat16 [256, 256], replicated, may hold values from -0.375 to 0.375
- coarse_qkv: bfloat16 [3, 1024, 1024], P(None, ('gy', 'gx')), may hold values from -0.1875 to 0.1875
- coarse_out: bfloat16 [1024, 1024], P(('gy', 'gx')), may hold values from -0.1875 to 0.1875
Outputs:
- dx_fine: bfloat16 [32, 32, 128, 256], P('batch', 'gy', 'gx')
- dx_coarse: bfloat16 [32, 16, 16, 1024], P('batch', 'gy', 'gx')
- grad_fine_qkv: bfloat16 [256, 768], replicated
- grad_fine_out: bfloat16 [256, 256], replicated
- grad_coarse_qkv: bfloat16 [3, 1024, 1024], P(None, ('gy', 'gx'))
- grad_coarse_out: bfloat16 [1024, 1024], P(('gy', 'gx'))
The draws below stay inside these ranges and needn't reach their ends.
Inputs may be any that keep to these rules, and one draw needn't show every extreme that they name: `fine_gain`: the norm gains are positive. `coarse_gain`: the norm gains are positive.
All inputs are finite; a program needn't handle non-finite values.
Results may differ from the reference program's by a relative error of at most 0.017.
The reference program's roundings to bfloat16 on the way count: a program that leaves them out, or rounds other values in their place, can miss the bound.
Values may be sent and summed in bfloat16 or wider, within the bound.
A program may use at most 64 MiB of HBM per device.

```python
import math
import jax
import jax.numpy as jnp
from jax import lax

D_F = 256
H_F = 4
D_C = 1024
H_C = 16
HD = 64
RAD = 3
BATCH = 32
ROWS_F = 32
COLS_F = 128
ROWS_C = 16
COLS_C = 16


def gain_law(key, channels):
    return jnp.clip(1.0 + 0.15 * jax.random.normal(key, (channels,), jnp.float32), 0.5, 1.5)


def draw_fine_gain(key, part):
    return gain_law(jax.random.fold_in(key, 11), D_F)


def draw_coarse_gain(key, part):
    return gain_law(jax.random.fold_in(key, 23), D_C)


def touch_ends(values, key, least, largest):
    shape = values.shape
    spot = [jax.random.randint(jax.random.fold_in(key, axis), (), 0, shape[axis]) for axis in range(len(shape))]
    values = values.at[tuple(spot)].set(least)
    longest = shape.index(max(shape))
    spot[longest] = (spot[longest] + 1) % shape[longest]
    return values.at[tuple(spot)].set(largest)


def block_levels(own_key, shape, split, low, largest):
    gain = 1.0
    for position, parts in split:
        steps = jax.random.uniform(jax.random.fold_in(jax.random.fold_in(own_key, 6), position), (parts,), jnp.float32, low / len(split), largest / len(split))
        gain = gain * jnp.repeat(jnp.exp(steps), shape[position] // parts).reshape((-1,) + (1,) * (len(shape) - 1 - position))
    return gain


def noise(rng, shape, deviation, reach, cuts=(), kind=jnp.bfloat16):
    drawn = deviation * jax.random.normal(rng, shape, jnp.float32)
    if cuts:
        drawn = drawn * block_levels(rng, shape, cuts, -0.22, 0.18)
    return jnp.clip(drawn, -reach, reach).astype(kind)


def setup_inputs(seed: int = 0) -> dict:
    key_list = jax.random.split(jax.random.key(seed), 12)
    x_fine = noise(key_list[0], (BATCH, ROWS_F, COLS_F, D_F), 1.0, 6.0, ((0, 32), (1, 4), (2, 4)))
    dy_fine = noise(key_list[1], (BATCH, ROWS_F, COLS_F, D_F), 1.0, 6.0, ((0, 32), (1, 4), (2, 4)))
    x_coarse = noise(key_list[2], (BATCH, ROWS_C, COLS_C, D_C), 1.0, 6.0, ((0, 32), (1, 4), (2, 4)))
    dy_coarse = noise(key_list[3], (BATCH, ROWS_C, COLS_C, D_C), 1.0, 6.0, ((0, 32), (1, 4), (2, 4)))
    timestep = touch_ends(jax.random.randint(key_list[4], (BATCH,), 0, 1000), jax.random.fold_in(key_list[4], 1), 0, 999).astype(jnp.int32)
    fine_gain = draw_fine_gain(jax.random.fold_in(key_list[11], 71), 0)
    coarse_gain = draw_coarse_gain(jax.random.fold_in(key_list[11], 71), 0)
    fine_qkv = noise(key_list[7], (D_F, 3 * D_F), D_F ** -0.5, 0.375)
    fine_out = noise(key_list[8], (D_F, D_F), D_F ** -0.5, 0.375)
    coarse_qkv = noise(key_list[9], (3, D_C, D_C), D_C ** -0.5, 0.1875, ((1, 16),))
    coarse_out = noise(key_list[10], (D_C, D_C), D_C ** -0.5, 0.1875, ((0, 16),))
    return {"x_fine": x_fine, "dy_fine": dy_fine, "x_coarse": x_coarse, "dy_coarse": dy_coarse, "timestep": timestep, "fine_gain": fine_gain, "coarse_gain": coarse_gain, "fine_qkv": fine_qkv, "fine_out": fine_out, "coarse_qkv": coarse_qkv, "coarse_out": coarse_out}


eps = 1e-06
log_span = math.log(1000.0)
block_side = 8

def contract(pattern, first_op, second_op):
    return jnp.einsum(pattern, first_op.astype(jnp.float32), second_op.astype(jnp.float32))

def score_scale():
    return 1.0 / math.sqrt(HD)

def time_gain(gains, step_value):
    channels = gains.shape[0]
    frequency = jnp.exp(-log_span * jnp.arange(channels, dtype=jnp.float32) / channels)
    return gains * (1.0 + 0.5 * jnp.cos(step_value.astype(jnp.float32) * frequency))

def norm_forward(source, factor):
    floats = source.astype(jnp.float32)
    inverse = lax.rsqrt(lax.optimization_barrier(jnp.mean(floats * floats, axis=-1, keepdims=True)) + eps)
    return ((floats * inverse * factor).astype(jnp.bfloat16), inverse)

def norm_backward(source, inverse, factor, upstream):
    floats = source.astype(jnp.float32)
    scaled = upstream * factor
    middle = lax.optimization_barrier(jnp.mean(floats * scaled, axis=-1, keepdims=True))
    return (inverse * scaled - floats * inverse * inverse * inverse * middle).astype(jnp.bfloat16)

def to_tiles(planar):
    height, breadth, channels = planar.shape
    pieces = planar.reshape(height // block_side, block_side, breadth // block_side, block_side, channels)
    return pieces.transpose(0, 2, 1, 3, 4).reshape(-1, block_side * block_side, channels)

def from_tiles(blocks, height, breadth):
    channels = blocks.shape[-1]
    pieces = blocks.reshape(height // block_side, breadth // block_side, block_side, block_side, channels)
    return pieces.transpose(0, 2, 1, 3, 4).reshape(height, breadth, channels)

def windows(padded, height, breadth):
    extent = block_side + 2 * RAD
    block_rows = height // block_side
    across = breadth // block_side
    channels = padded.shape[-1]
    widened = jnp.pad(padded, ((0, (block_rows + 1) * block_side - padded.shape[0]), (0, (across + 1) * block_side - padded.shape[1]), (0, 0)))
    blocks_grid = widened.reshape(block_rows + 1, block_side, across + 1, block_side, channels).transpose(0, 2, 1, 3, 4)
    upper_pair = jnp.concatenate([blocks_grid[:-1, :-1], blocks_grid[:-1, 1:]], axis=3)
    lower_pair = jnp.concatenate([blocks_grid[1:, :-1], blocks_grid[1:, 1:]], axis=3)
    square = jnp.concatenate([upper_pair, lower_pair], axis=2)
    return square[:, :, :extent, :extent].reshape(block_rows * across, extent * extent, channels)

def intersection_add(windowed, height, breadth):
    extent = block_side + 2 * RAD
    block_rows = height // block_side
    across = breadth // block_side
    channels = windowed.shape[-1]
    layout = windowed.reshape(block_rows, across, extent, extent, channels)
    layout = jnp.pad(layout, ((0, 0), (0, 0), (0, 2 * block_side - extent), (0, 2 * block_side - extent), (0, 0)))
    summed = jnp.zeros((block_rows + 1, across + 1, block_side, block_side, channels), jnp.float32)
    for row_half in range(2):
        for col_half in range(2):
            quarter = layout[:, :, row_half * block_side:(row_half + 1) * block_side, col_half * block_side:(col_half + 1) * block_side]
            summed = summed + jnp.pad(quarter, ((row_half, 1 - row_half), (col_half, 1 - col_half), (0, 0), (0, 0), (0, 0)))
    merged = summed.transpose(0, 2, 1, 3, 4).reshape((block_rows + 1) * block_side, (across + 1) * block_side, channels)
    return merged[:height + 2 * RAD, :breadth + 2 * RAD]

def pair_mask():
    extent = block_side + 2 * RAD
    inner_pos = jnp.arange(block_side * block_side)
    outer_pos = jnp.arange(extent * extent)
    row_gap = outer_pos[None, :] // extent - inner_pos[:, None] // block_side
    col_gap = outer_pos[None, :] % extent - inner_pos[:, None] % block_side
    return (row_gap >= 0) & (row_gap <= 2 * RAD) & (col_gap >= 0) & (col_gap <= 2 * RAD)

def fine_forward(queries, key_values, valid_pad):
    height, breadth, channels = queries.shape
    query_blocks = to_tiles(queries)
    block_count = query_blocks.shape[0]
    query_heads = query_blocks.reshape(block_count, -1, H_F, HD)
    key_windows = windows(key_values, height, breadth)
    key_heads = key_windows[..., :channels].reshape(block_count, -1, H_F, HD)
    value_heads = key_windows[..., channels:].reshape(block_count, -1, H_F, HD)
    allowed = pair_mask()[None, None] & windows(valid_pad[..., None], height, breadth)[:, None, None, :, 0]
    scores = contract('bqhe,bkhe->bhqk', query_heads, key_heads) * score_scale()
    scores = jnp.where(allowed, scores, -1e+30)
    peak = lax.optimization_barrier(jnp.max(scores, axis=-1, keepdims=True))
    log_total = peak + jnp.log(lax.optimization_barrier(jnp.sum(jnp.exp(scores - peak), axis=-1, keepdims=True)))
    shares = jnp.where(allowed, jnp.exp(scores - log_total), 0.0)
    weights = shares.astype(jnp.bfloat16)
    mixed = contract('bhqk,bkhe->bqhe', weights, value_heads).astype(jnp.bfloat16)
    attended = from_tiles(mixed.reshape(block_count, -1, channels), height, breadth)
    return (attended, query_heads, key_heads, value_heads, shares, weights, log_total)

def fine_query_backward(upstream, query_heads, key_heads, value_heads, shares, height, breadth):
    block_count = query_heads.shape[0]
    upward_heads = to_tiles(upstream).reshape(block_count, -1, H_F, HD)
    products = contract('bqhe,bkhe->bhqk', upward_heads, value_heads)
    centre = lax.optimization_barrier(jnp.sum(shares * products, axis=-1, keepdims=True))
    slopes = (shares * (products - centre)).astype(jnp.bfloat16)
    grad_query = contract('bhqk,bkhe->bqhe', slopes, key_heads) * score_scale()
    grad_query = from_tiles(grad_query.reshape(block_count, -1, H_F * HD), height, breadth)
    return (grad_query, upward_heads, slopes, centre)

def key_grads_windows(slopes, weights, query_heads, upward_heads):
    block_count = query_heads.shape[0]
    grad_key = contract('bhqk,bqhe->bkhe', slopes, query_heads).reshape(block_count, -1, D_F)
    grad_value = contract('bhqk,bqhe->bkhe', weights, upward_heads).reshape(block_count, -1, D_F)
    return jnp.concatenate([grad_key, grad_value], axis=-1)

def fine_image(picture, cotangent, step_value, gains, fine_qkv, fine_out):
    height, breadth = (picture.shape[0], picture.shape[1])
    factor = time_gain(gains, step_value)
    normed, inverse = norm_forward(picture, factor)
    flat_normed = normed.reshape(-1, D_F)
    projected = jnp.dot(flat_normed, fine_qkv, preferred_element_type=jnp.float32).astype(jnp.bfloat16).reshape(height, breadth, 3 * D_F)
    queries = projected[..., :D_F]
    key_values = jnp.pad(projected[..., D_F:], ((RAD, RAD), (RAD, RAD), (0, 0)))
    valid_pad = jnp.pad(jnp.ones((height, breadth), dtype=jnp.bool_), RAD)
    attended, query_heads, key_heads, value_heads, shares, weights, log_total = fine_forward(queries, key_values, valid_pad)
    flat_cot = cotangent.reshape(-1, D_F)
    grad_out = jnp.dot(attended.reshape(-1, D_F).T, flat_cot, preferred_element_type=jnp.float32)
    upstream = jnp.dot(flat_cot, fine_out.T, preferred_element_type=jnp.float32).astype(jnp.bfloat16).reshape(height, breadth, D_F)
    grad_query, upward_heads, slopes, centre = fine_query_backward(upstream, query_heads, key_heads, value_heads, shares, height, breadth)
    padded_grads = intersection_add(key_grads_windows(slopes, weights, query_heads, upward_heads), height, breadth)
    key_grads = padded_grads[RAD:RAD + height, RAD:RAD + breadth]
    grad_proj = jnp.concatenate([grad_query, key_grads[..., :D_F] * score_scale(), key_grads[..., D_F:]], axis=-1).astype(jnp.bfloat16).reshape(-1, 3 * D_F)
    grad_qkv = jnp.dot(flat_normed.T, grad_proj, preferred_element_type=jnp.float32)
    down_grad = jnp.dot(grad_proj, fine_qkv.T, preferred_element_type=jnp.float32).reshape(height, breadth, D_F)
    return (norm_backward(picture, inverse, factor, down_grad), grad_qkv, grad_out)

def coarse_image(picture, cotangent, step_value, gains, coarse_qkv, coarse_out):
    tokens = picture.reshape(-1, D_C)
    factor = time_gain(gains, step_value)
    normed, inverse = norm_forward(tokens, factor)
    qkv_heads = coarse_qkv.reshape(3, H_C, HD, D_C)
    out_heads = coarse_out.reshape(H_C, HD, D_C)
    projected = contract('td,khed->khte', normed, qkv_heads).astype(jnp.bfloat16)
    queries, keys, values = (projected[0], projected[1], projected[2])
    scores = contract('hte,hse->hts', queries, keys) * score_scale()
    peak = lax.optimization_barrier(jnp.max(scores, axis=-1, keepdims=True))
    log_total = peak + jnp.log(lax.optimization_barrier(jnp.sum(jnp.exp(scores - peak), axis=-1, keepdims=True)))
    shares = jnp.exp(scores - log_total)
    weights = shares.astype(jnp.bfloat16)
    mixed = contract('hts,hse->hte', weights, values).astype(jnp.bfloat16)
    flat_cot = cotangent.reshape(-1, D_C)
    upstream = contract('td,hed->hte', flat_cot, out_heads).astype(jnp.bfloat16)
    grad_out = contract('hte,td->hed', mixed, flat_cot).reshape(D_C, D_C)
    products = contract('hte,hse->hts', upstream, values)
    centre = lax.optimization_barrier(jnp.sum(shares * products, axis=-1, keepdims=True))
    slopes = (shares * (products - centre)).astype(jnp.bfloat16)
    grad_query = (contract('hts,hse->hte', slopes, keys) * score_scale()).astype(jnp.bfloat16)
    grad_key = (contract('hts,hte->hse', slopes, queries) * score_scale()).astype(jnp.bfloat16)
    grad_value = contract('hts,hte->hse', weights, upstream).astype(jnp.bfloat16)
    stacked = jnp.stack([grad_query, grad_key, grad_value])
    grad_qkv = contract('khte,td->khed', stacked, normed).reshape(3, D_C, D_C)
    head_parts = contract('khte,khed->htd', stacked, qkv_heads).astype(jnp.bfloat16)
    down_grad = lax.optimization_barrier(jnp.sum(head_parts.astype(jnp.float32), axis=0))
    return (norm_backward(tokens, inverse, factor, down_grad).reshape(picture.shape), grad_qkv, grad_out)

def reference(x_fine, dy_fine, x_coarse, dy_coarse, timestep, fine_gain, coarse_gain, fine_qkv, fine_out, coarse_qkv, coarse_out):

    def one_image(running, inputs):
        picture, cotangent, coarse_picture, coarse_cot, step_value = inputs
        dx_picture, grad_fq, grad_fo = fine_image(picture, cotangent, step_value, fine_gain, fine_qkv, fine_out)
        dx_coarse_pic, grad_cq, grad_co = coarse_image(coarse_picture, coarse_cot, step_value, coarse_gain, coarse_qkv, coarse_out)
        updated = (running[0] + grad_fq, running[1] + grad_fo, running[2] + grad_cq, running[3] + grad_co)
        return (updated, (dx_picture, dx_coarse_pic))
    start = (jnp.zeros((D_F, 3 * D_F), jnp.float32), jnp.zeros((D_F, D_F), jnp.float32), jnp.zeros((3, D_C, D_C), jnp.float32), jnp.zeros((D_C, D_C), jnp.float32))
    sums, outputs = lax.scan(one_image, start, (x_fine, dy_fine, x_coarse, dy_coarse, timestep))
    return (outputs[0], outputs[1], sums[0].astype(jnp.bfloat16), sums[1].astype(jnp.bfloat16), sums[2].astype(jnp.bfloat16), sums[3].astype(jnp.bfloat16))
```

```python
import math

import jax
import jax.numpy as jnp
from jax import lax
from jax.experimental import pallas as pl
from jax.experimental.pallas import tpu as pltpu
from jax.sharding import PartitionSpec as P

D_F = 256
H_F = 4
D_C = 1024
HD = 64
RAD = 3
F32 = jnp.float32
BF16 = jnp.bfloat16
MESH = pl.DeviceIdType.MESH

eps = 1e-06
log_span = math.log(1000.0)
scale = 1.0 / math.sqrt(HD)

OWN, LEFT, RIGHT, TOP, BOTTOM, TL, TR, BL, BR = range(9)
SEGMENTS = (
    (0, 8, 32, 0, 0),
    (256, 8, 8, 0, -8),
    (320, 8, 8, 0, 32),
    (384, 3, 32, -3, 0),
    (480, 3, 32, 8, 0),
    (576, 4, 8, -4, -8),
    (608, 4, 8, -4, 32),
    (640, 4, 8, 8, -8),
    (672, 4, 8, 8, 32),
)
KEYS = 704
HALO = KEYS - 256
FROM = {LEFT: (0, -1), RIGHT: (0, 1), TOP: (-1, 0), BOTTOM: (1, 0),
        TL: (-1, -1), TR: (-1, 1), BL: (1, -1), BR: (1, 1)}
BACK = {LEFT: RIGHT, RIGHT: LEFT, TOP: BOTTOM, BOTTOM: TOP, TL: BR, BR: TL, TR: BL, BL: TR}


def nn(a, b):
    return lax.dot_general(a, b, (((1,), (0,)), ((), ())), preferred_element_type=F32)


def nt(a, b):
    return lax.dot_general(a, b, (((1,), (1,)), ((), ())), preferred_element_type=F32)


def tn(a, b):
    return lax.dot_general(a, b, (((0,), (0,)), ((), ())), preferred_element_type=F32)


def rcopy(src, dst, ssem, rsem, device):
    return pltpu.make_async_remote_copy(
        src_ref=src, dst_ref=dst, send_sem=ssem, recv_sem=rsem,
        device_id=device, device_id_type=MESH,
    )


def time_gain(gains, step_value):
    channels = gains.shape[0]
    frequency = jnp.exp(-log_span * jnp.arange(channels, dtype=F32) / channels)
    return gains * (1.0 + 0.5 * jnp.cos(step_value.astype(F32) * frequency))


def norm_backward(floats, inverse, factor, upstream):
    scaled = upstream * factor
    middle = jnp.mean(floats * scaled, axis=-1, keepdims=True)
    return (inverse * scaled - floats * inverse * inverse * inverse * middle).astype(BF16)


def kernel(
    xf, dyf, xc, dyc, ff, fc, wqkv, wout, cw, cwo,
    dxf, dxc, gfq, gfo, gcq, gco,
    ag, kv, edge, bias, nf, qm, um, kt, vt, wall, sall, att, dqt, dkv, gsend, grecv,
    rs_send, rsx, rsz_send, rsz,
    cg, cgb, cgp, c16, c16r, cfin,
    fg, fgb, fgp, f16, f16r, fone, ffin,
    s_ag, r_ag, s_h, r_h, s_g, r_g, s_rx, r_rx, s_rz, r_rz,
    s_cc, r_cc, s_c16, r_c16, s_cag, r_cag,
    s_fc, r_fc, s_f16, r_f16, s_f1, r_f1, s_fag, r_fag,
):
    b = lax.axis_index("batch")
    gy = lax.axis_index("gy")
    gx = lax.axis_index("gx")
    core = lax.rem(b, 2)
    bz = b // 2
    slot = gx * 4 + gy

    def group(p):
        return (b, lax.rem(p, 4), p // 4)

    def batch(p):
        return (p * 2 + core, gy, gx)

    partner = (b + 1 - 2 * core, gy, gx)

    barrier = pltpu.get_barrier_semaphore()

    def greet(i, carry):
        pl.semaphore_signal(barrier, inc=1, device_id=group(lax.rem(slot + i, 16)), device_id_type=MESH)
        pl.semaphore_signal(barrier, inc=1, device_id=batch(lax.rem(bz + i, 16)), device_id_type=MESH)
        return carry

    lax.fori_loop(1, 16, greet, 0)
    pl.semaphore_signal(barrier, inc=1, device_id=partner, device_id_type=MESH)

    xcf = xc[...].astype(F32)
    inv_c = lax.rsqrt(jnp.mean(xcf * xcf, axis=-1, keepdims=True) + eps)
    ag[slot, 0:16, :] = (xcf * inv_c * fc[...]).astype(BF16)
    ag[slot, 16:32, :] = dyc[...]

    xff = xf[...].astype(F32)
    inv_f = lax.rsqrt(jnp.mean(xff * xff, axis=-1, keepdims=True) + eps)
    normed = (xff * inv_f * ff[...]).astype(BF16)
    nf[...] = normed
    kvp = nn(normed, wqkv[:, 256:768])
    kv[0:256, :] = kvp.astype(BF16)
    kvp3 = kvp.reshape(8, 32, 512)
    edge[0, :, :] = kvp3[:, 0:8, :].reshape(64, 512).astype(BF16)
    edge[1, :, :] = kvp3[:, 24:32, :].reshape(64, 512).astype(BF16)

    pl.semaphore_wait(barrier, 31)

    src = {
        LEFT: edge.at[1], RIGHT: edge.at[0],
        TOP: kv.at[pl.ds(160, 96)], BOTTOM: kv.at[pl.ds(0, 96)],
        TL: edge.at[1, pl.ds(32, 32)], TR: edge.at[0, pl.ds(32, 32)],
        BL: edge.at[1, pl.ds(0, 32)], BR: edge.at[0, pl.ds(0, 32)],
    }

    def toward(step):
        return (b, lax.rem(gy + step[0] + 4, 4), lax.rem(gx + step[1] + 4, 4))

    def size(s):
        return SEGMENTS[s][1] * SEGMENTS[s][2]

    halo = []
    for s in range(1, 9):
        dy, dx = FROM[s]
        halo.append(rcopy(src[s], kv.at[pl.ds(SEGMENTS[s][0], size(s))], s_h.at[s - 1], r_h.at[s - 1],
                          toward((-dy, -dx))))

    up, down, opp = lax.rem(gy + 1, 4), lax.rem(gy + 3, 4), lax.rem(gy + 2, 4)
    right, left, far = lax.rem(gx + 1, 4), lax.rem(gx + 3, 4), lax.rem(gx + 2, 4)
    to_up, to_down = (b, up, gx), (b, down, gx)
    to_right, to_left = (b, gy, right), (b, gy, left)
    sends = []

    def ag_send(g, x, part, device):
        sl = x * 4 + g
        block = ag.at[sl] if part is None else ag.at[sl, pl.ds(16 * part, 16)]
        c = rcopy(block, block, s_ag.at[len(sends)], r_ag.at[sl, part or 0], device)
        c.start()
        sends.append(c)

    def ag_wait(g, x, part=None):
        sl = x * 4 + g
        block = ag.at[sl] if part is None else ag.at[sl, pl.ds(16 * part, 16)]
        rcopy(block, block, s_ag.at[0], r_ag.at[sl, part or 0], to_up).wait_recv()

    ag_send(gy, gx, None, to_up)
    ag_send(gy, gx, None, to_down)
    for s in (TOP, BOTTOM, LEFT, RIGHT, TL, TR, BL, BR):
        halo[s - 1].start()
    ag_send(gy, gx, None, to_right)
    ag_send(gy, gx, None, to_left)

    q = nn(normed, wqkv[:, 0:256])
    upst = nt(dyf[...], wout[...])
    lane = lax.broadcasted_iota(jnp.int32, (256, 256), 1) // HD
    for h in range(H_F):
        qm[h * 256:(h + 1) * 256, :] = jnp.where(lane == h, q, 0.0).astype(BF16)
        um[h * 256:(h + 1) * 256, :] = jnp.where(lane == h, upst, 0.0).astype(BF16)
    ok_side = {OWN: None, LEFT: gx > 0, RIGHT: gx < 3, TOP: gy > 0, BOTTOM: gy < 3,
               TL: (gx > 0) & (gy > 0), TR: (gx < 3) & (gy > 0),
               BL: (gx > 0) & (gy < 3), BR: (gx < 3) & (gy < 3)}
    for s, (first, rows, cols, row0, col0) in enumerate(SEGMENTS):
        n = rows * cols
        key = lax.broadcasted_iota(jnp.int32, (n, 256), 0)
        query = lax.broadcasted_iota(jnp.int32, (n, 256), 1)
        dr = key // cols + row0 - query // 32
        dc = lax.rem(key, cols) + col0 - lax.rem(query, 32)
        ok = (dr >= -RAD) & (dr <= RAD) & (dc >= -RAD) & (dc <= RAD)
        floor = jnp.where(ok, 0.0, -1e30).astype(F32)
        if ok_side[s] is not None:
            floor = jnp.minimum(floor, jnp.where(ok_side[s], 0.0, -1e30).astype(F32))
        bias[first:first + n, :] = floor

    def relay_near():
        ag_wait(down, gx)
        ag_send(down, gx, 0, to_up)
        ag_send(down, gx, None, to_right)
        ag_send(down, gx, None, to_left)
        ag_wait(up, gx)
        ag_send(up, gx, 1, to_down)
        ag_send(up, gx, None, to_right)
        ag_send(up, gx, None, to_left)
        ag_wait(gy, left)
        ag_send(gy, left, 0, to_right)
        ag_wait(gy, right)
        ag_send(gy, right, 1, to_left)

    def relay_opposite():
        ag_wait(opp, gx, 0)
        ag_wait(opp, gx, 1)
        ag_send(opp, gx, None, to_right)
        ag_send(opp, gx, None, to_left)

    def relay_side():
        for g in (down, up):
            ag_wait(g, left)
            ag_send(g, left, 0, to_right)
            ag_wait(g, right)
            ag_send(g, right, 1, to_left)

    def relay_last():
        ag_wait(opp, left)
        ag_send(opp, left, 0, to_right)
        ag_wait(opp, right)
        ag_send(opp, right, 1, to_left)

    relay_near()
    for c in halo:
        c.wait_recv()

    kt[...] = kv[:, 0:256].T
    vt[...] = kv[:, 256:512].T

    relays = (relay_opposite, relay_side, relay_last, lambda: None)
    for h in range(H_F):
        rows = slice(h * 64, (h + 1) * 64)
        heads = slice(h * 256, (h + 1) * 256)
        s = nt(kv[:, 0:256], qm[heads, :]) * scale + bias[...]
        top = jnp.max(s, axis=0, keepdims=True)
        e = jnp.exp(s - top)
        p = e * (1.0 / jnp.sum(e, axis=0, keepdims=True))
        w = p.astype(BF16)
        wall[:, heads] = w
        dp = nt(kv[:, 256:512], um[heads, :])
        delta = jnp.sum(p * dp, axis=0, keepdims=True)
        slope = (p * (dp - delta)).astype(BF16)
        sall[:, heads] = slope
        att[rows, :] = nn(vt[rows, :], w).astype(BF16)
        dqt[rows, :] = nn(kt[rows, :], slope) * scale
        relays[h]()

    gsend[:, 0:256] = nn(sall[256:KEYS, :], qm[...]).astype(BF16)
    gsend[:, 256:512] = nn(wall[256:KEYS, :], um[...]).astype(BF16)
    ghalo = []
    for s in range(1, 9):
        dy, dx = FROM[s]
        o = BACK[s]
        c = rcopy(gsend.at[pl.ds(SEGMENTS[s][0] - 256, size(s))],
                  grecv.at[pl.ds(SEGMENTS[o][0] - 256, size(o))],
                  s_g.at[s - 1], r_g.at[s - 1], toward((dy, dx)))
        c.start()
        ghalo.append(c)
    dkv[:, :, 0:256] = nn(sall[0:256, :], qm[...]).reshape(8, 32, 256)
    dkv[:, :, 256:512] = nn(wall[0:256, :], um[...]).reshape(8, 32, 256)
    fgo = nn(att[...], dyf[...])

    for g in range(4):
        ag_wait(g, far, 0)
        ag_wait(g, far, 1)
    nall = ag[:, 0:16, :].reshape(256, D_C)
    call = ag[:, 16:32, :].reshape(256, D_C)
    proj = nt(cw[...], nall).astype(BF16)
    cqt, ckt, cvt = proj[0:64], proj[64:128], proj[128:192]
    cut = nt(cwo[...], call).astype(BF16)
    cs = tn(ckt, cqt) * scale
    ce = jnp.exp(cs - jnp.max(cs, axis=0, keepdims=True))
    cp = ce * (1.0 / jnp.sum(ce, axis=0, keepdims=True))
    cwt = cp.astype(BF16)
    cot = nn(cvt, cwt).astype(BF16)
    cdp = tn(cvt, cut)
    cdelta = jnp.sum(cp * cdp, axis=0, keepdims=True)
    cslope = (cp * (cdp - cdelta)).astype(BF16)
    cdt = jnp.concatenate(
        [nn(ckt, cslope) * scale, nt(cqt, cslope) * scale, nt(cut, cwt)], axis=0
    ).astype(BF16)
    rs_send[...] = tn(cdt, cw[...]).astype(BF16).reshape(4, 4, 16, D_C)
    rx = []
    for i in (1, 3, 2):
        x = lax.rem(gx + i, 4)
        c = rcopy(rs_send.at[x], rsx.at[i], s_rx.at[i], r_rx.at[i], (b, gy, x))
        c.start()
        rx.append(c)
    cgq = nn(cdt, nall)
    cgo = nn(cot, call)
    for half in range(2):
        lanes = slice(half * 512, (half + 1) * 512)
        cg[half, 0:192, :] = cgq[:, lanes]
        cg[half, 192:256, :] = cgo[:, lanes]
        cgb[half, 0:192, :] = cgq[:, lanes].astype(BF16)
        cgb[half, 192:256, :] = cgo[:, lanes].astype(BF16)
    cc = rcopy(cgb.at[1 - core], cgp, s_cc.at[0], r_cc.at[0], partner)
    cc.start()

    for c in ghalo:
        c.wait_recv()

    def owed(s):
        first, rows, cols = SEGMENTS[s][:3]
        return grecv[first - 256:first - 256 + rows * cols, :].astype(F32).reshape(rows, cols, 512)

    dkv[:, 0:8, :] += owed(LEFT)
    dkv[:, 24:32, :] += owed(RIGHT)
    dkv[0:3, :, :] += owed(TOP)
    dkv[5:8, :, :] += owed(BOTTOM)
    dkv[0:4, 0:8, :] += owed(TL)
    dkv[0:4, 24:32, :] += owed(TR)
    dkv[4:8, 0:8, :] += owed(BL)
    dkv[4:8, 24:32, :] += owed(BR)
    dq = dqt[...].T.astype(BF16)
    dk = (dkv[:, :, 0:256].reshape(256, 256) * scale).astype(BF16)
    dv = dkv[:, :, 256:512].reshape(256, 256).astype(BF16)
    nft = nf[...].T
    fgq = nn(nft, dq)
    fgk = nn(nft, dk)
    fgv = nn(nft, dv)
    for half, (a, z) in enumerate(((fgq, fgk), (fgv, fgo))):
        fg[half, :, 0:256] = a
        fg[half, :, 256:512] = z
        fgb[half, :, 0:256] = a.astype(BF16)
        fgb[half, :, 256:512] = z.astype(BF16)
    fcc = rcopy(fgb.at[1 - core], fgp, s_fc.at[0], r_fc.at[0], partner)
    fcc.start()
    dn = nt(dq, wqkv[:, 0:256]) + nt(dk, wqkv[:, 256:512]) + nt(dv, wqkv[:, 512:768])
    xff = xf[...].astype(F32)
    inv_f = lax.rsqrt(jnp.mean(xff * xff, axis=-1, keepdims=True) + eps)
    dxf[...] = norm_backward(xff, inv_f, ff[...], dn)

    def spread(source, dest, ssem, rsem, me, device, each):
        def body(i, carry):
            p = lax.rem(me + i, 16)
            rcopy(source.at[p] if each else source, dest.at[me], ssem.at[i], rsem.at[me], device(p)).start()
            return carry
        lax.fori_loop(1, 16, body, 0)

    def collect(source, dest, ssem, rsem, me, device, each):
        def body(i, carry):
            p = lax.rem(me + i, 16)
            c = rcopy(source.at[p] if each else source, dest.at[p], ssem.at[i], rsem.at[p], device(p))
            c.wait_send()
            c.wait_recv()
            return carry
        lax.fori_loop(1, 16, body, 0)

    def total(dest):
        acc = dest[0].astype(F32)
        for i in range(1, 16):
            acc = acc + dest[i].astype(F32)
        return acc

    cc.wait_recv()
    c16[...] = (cg[core] + cgp[...].astype(F32)).astype(BF16).reshape(16, 16, 512)
    c16r[bz] = c16[bz]
    spread(c16, c16r, s_c16, r_c16, bz, batch, True)

    fcc.wait_recv()
    f16[...] = (fg[core] + fgp[...].astype(F32)).astype(BF16).reshape(16, 16, 512)
    f16r[slot] = f16[slot]
    spread(f16, f16r, s_f16, r_f16, slot, group, True)

    acc = rs_send[gx].astype(F32)
    for i, c in zip((1, 3, 2), rx):
        c.wait_recv()
        acc = acc + rsx[i].astype(F32)
    rsz_send[...] = acc.astype(BF16)
    rz = []
    for i in (1, 3, 2):
        g = lax.rem(gy + i, 4)
        c = rcopy(rsz_send.at[g], rsz.at[i], s_rz.at[i], r_rz.at[i], (b, g, gx))
        c.start()
        rz.append(c)

    collect(c16, c16r, s_c16, r_c16, bz, batch, True)
    cmine = cfin.at[core, bz]
    cmine[...] = total(c16r).astype(BF16)
    spread(cmine, cfin.at[core], s_cag, r_cag, bz, batch, False)

    collect(f16, f16r, s_f16, r_f16, slot, group, True)
    fone[bz] = total(f16r).astype(BF16)
    spread(fone.at[bz], fone, s_f1, r_f1, bz, batch, False)

    dnc = rsz_send[gy].astype(F32)
    for i, c in zip((1, 3, 2), rz):
        c.wait_recv()
        dnc = dnc + rsz[i].astype(F32)
    xcf = xc[...].astype(F32)
    inv_c = lax.rsqrt(jnp.mean(xcf * xcf, axis=-1, keepdims=True) + eps)
    dxc[...] = norm_backward(xcf, inv_c, fc[...], dnc)

    collect(cmine, cfin.at[core], s_cag, r_cag, bz, batch, False)
    cc2 = rcopy(cfin.at[core], cfin.at[core], s_cc.at[1], r_cc.at[1], partner)
    cc2.start()

    collect(fone.at[bz], fone, s_f1, r_f1, bz, batch, False)
    fmine = ffin.at[core, slot]
    fmine[...] = total(fone).astype(BF16)
    spread(fmine, ffin.at[core], s_fag, r_fag, slot, group, False)

    rcopy(cfin.at[1 - core], cfin.at[1 - core], s_cc.at[1], r_cc.at[1], partner).wait_recv()
    for half in range(2):
        lanes = slice(half * 512, (half + 1) * 512)
        done = cfin[half].reshape(256, 512)
        gcq[:, lanes] = done[0:192]
        gco[:, lanes] = done[192:256]

    collect(fmine, ffin.at[core], s_fag, r_fag, slot, group, False)
    fc2 = rcopy(ffin.at[core], ffin.at[core], s_fc.at[1], r_fc.at[1], partner)
    fc2.start()
    rcopy(ffin.at[1 - core], ffin.at[1 - core], s_fc.at[1], r_fc.at[1], partner).wait_recv()
    gfq[:, 0:512] = ffin[0].reshape(256, 512)
    done = ffin[1].reshape(256, 512)
    gfq[:, 512:768] = done[:, 0:256]
    gfo[...] = done[:, 256:512]

    for c in sends + halo + ghalo + rx + rz + [cc, fcc, cc2, fc2]:
        c.wait_send()


def local(x_fine, dy_fine, x_coarse, dy_coarse, timestep, fine_gain, coarse_gain,
          fine_qkv, fine_out, coarse_qkv, coarse_out):
    t = timestep[0]
    vm = pl.BlockSpec(memory_space=pltpu.VMEM)
    dma = pltpu.SemaphoreType.DMA
    V = pltpu.VMEM
    outs = (
        jax.ShapeDtypeStruct((256, 256), BF16),
        jax.ShapeDtypeStruct((16, D_C), BF16),
        jax.ShapeDtypeStruct((256, 768), BF16),
        jax.ShapeDtypeStruct((256, 256), BF16),
        jax.ShapeDtypeStruct((192, D_C), BF16),
        jax.ShapeDtypeStruct((64, D_C), BF16),
    )
    scratch = [
        V((16, 32, D_C), BF16), V((KEYS, 512), BF16), V((2, 64, 512), BF16), V((KEYS, 256), F32),
        V((256, 256), BF16), V((1024, 256), BF16), V((1024, 256), BF16),
        V((256, KEYS), BF16), V((256, KEYS), BF16), V((KEYS, 1024), BF16), V((KEYS, 1024), BF16),
        V((256, 256), BF16), V((256, 256), F32), V((8, 32, 512), F32),
        V((HALO, 512), BF16), V((HALO, 512), BF16),
        V((4, 4, 16, D_C), BF16), V((4, 4, 16, D_C), BF16), V((4, 16, D_C), BF16), V((4, 16, D_C), BF16),
        V((2, 256, 512), F32), V((2, 256, 512), BF16), V((256, 512), BF16),
        V((16, 16, 512), BF16), V((16, 16, 512), BF16), V((2, 16, 16, 512), BF16),
        V((2, 256, 512), F32), V((2, 256, 512), BF16), V((256, 512), BF16),
        V((16, 16, 512), BF16), V((16, 16, 512), BF16), V((16, 16, 512), BF16), V((2, 16, 16, 512), BF16),
        dma((24,)), dma((16, 2)), dma((8,)), dma((8,)), dma((8,)), dma((8,)),
        dma((4,)), dma((4,)), dma((4,)), dma((4,)),
        dma((2,)), dma((2,)), dma((16,)), dma((16,)), dma((16,)), dma((16,)),
        dma((2,)), dma((2,)), dma((16,)), dma((16,)), dma((16,)), dma((16,)), dma((16,)), dma((16,)),
    ]
    dxf, dxc, gfq, gfo, gcq, gco = pl.pallas_call(
        kernel,
        out_shape=outs,
        in_specs=[vm] * 10,
        out_specs=[vm] * 6,
        scratch_shapes=scratch,
        compiler_params=pltpu.CompilerParams(
            collective_id=0, has_side_effects=True, vmem_limit_bytes=50 * 1024 * 1024
        ),
    )(
        x_fine.reshape(256, D_F), dy_fine.reshape(256, D_F),
        x_coarse.reshape(16, D_C), dy_coarse.reshape(16, D_C),
        time_gain(fine_gain, t)[None], time_gain(coarse_gain, t)[None],
        fine_qkv, fine_out, coarse_qkv.reshape(192, D_C), coarse_out,
    )
    return (
        dxf.reshape(x_fine.shape),
        dxc.reshape(x_coarse.shape),
        gfq,
        gfo,
        gcq.reshape(coarse_qkv.shape),
        gco,
    )


def solution(mesh):
    tile = P("batch", "gy", "gx", None)
    heads = P(None, ("gy", "gx"), None)
    rows = P(("gy", "gx"), None)
    return jax.shard_map(
        local,
        mesh=mesh,
        in_specs=(tile, tile, tile, tile, P("batch"), P(), P(), P(), P(), heads, rows),
        out_specs=(tile, tile, P(), P(), heads, rows),
        check_vma=False,
    )
```

```python
import math

import jax
import jax.numpy as jnp
from jax import lax
from jax.experimental import pallas as pl
from jax.experimental.pallas import tpu as pltpu
from jax.sharding import PartitionSpec as P

D_F = 256
H_F = 4
D_C = 1024
HD = 64
RAD = 3
F32 = jnp.float32
BF16 = jnp.bfloat16
MESH = pl.DeviceIdType.MESH

eps = 1e-06
log_span = math.log(1000.0)
scale = 1.0 / math.sqrt(HD)

OWN, LEFT, RIGHT, TOP, BOTTOM, TL, TR, BL, BR = range(9)
SEGMENTS = (
    (0, 8, 32, 0, 0),
    (256, 8, 8, 0, -8),
    (320, 8, 8, 0, 32),
    (384, 3, 32, -3, 0),
    (480, 3, 32, 8, 0),
    (576, 4, 8, -4, -8),
    (608, 4, 8, -4, 32),
    (640, 4, 8, 8, -8),
    (672, 4, 8, 8, 32),
)
KEYS = 704
HALO = KEYS - 256
FROM = {LEFT: (0, -1), RIGHT: (0, 1), TOP: (-1, 0), BOTTOM: (1, 0),
        TL: (-1, -1), TR: (-1, 1), BL: (1, -1), BR: (1, 1)}
BACK = {LEFT: RIGHT, RIGHT: LEFT, TOP: BOTTOM, BOTTOM: TOP, TL: BR, BR: TL, TR: BL, BL: TR}


def nn(a, b):
    return lax.dot_general(a, b, (((1,), (0,)), ((), ())), preferred_element_type=F32)


def nt(a, b):
    return lax.dot_general(a, b, (((1,), (1,)), ((), ())), preferred_element_type=F32)


def tn(a, b):
    return lax.dot_general(a, b, (((0,), (0,)), ((), ())), preferred_element_type=F32)


def mark(name):
    pass


def rcopy(src, dst, ssem, rsem, device):
    return pltpu.make_async_remote_copy(
        src_ref=src, dst_ref=dst, send_sem=ssem, recv_sem=rsem,
        device_id=device, device_id_type=MESH,
    )


def time_gain(gains, step_value):
    channels = gains.shape[1]
    place = lax.broadcasted_iota(jnp.int32, (8, channels), 1).astype(F32)
    frequency = jnp.exp(-log_span * place / channels)
    factor = jnp.cos(step_value * frequency)
    return gains * (1.0 + 0.5 * factor[0:1])


def norm_backward(floats, inverse, factor, upstream):
    scaled = upstream * factor
    middle = jnp.mean(floats * scaled, axis=-1, keepdims=True)
    return (inverse * scaled - floats * inverse * inverse * inverse * middle).astype(BF16)


def kernel(
    t_ref, xf_h, dyf_h, xc_h, dyc_h, gf_h, gc_h, wqkv_h, wout_h, cw_h, cwo_h,
    dxf, dxc, gfq, gfo, gcq, gco,
    xf, dyf, xc4, dyc4, gf, gc, wqkv, wout, cw, cwo, xc, ff, fc,
    ag, nrm, kv, edge, bias, qm, um, kt, vt, nt_all, wall, sall, att, dqt, dn, gsend, grecv,
    rs_send, rsx, rsz_send, rsz,
    cg, cgb, cgp, c16, c16r, cfin,
    fg, fgb, fgp, f16, f16r, fone, ffin,
    s_in, s_ag, r_ag, s_h, r_h, s_g, r_g, s_rx, r_rx, s_rz, r_rz,
    s_cc, r_cc, s_c16, r_c16, s_cag, r_cag, s_cf, r_cf,
    s_fc, r_fc, s_f16, r_f16, s_f1, r_f1, s_fag, r_fag, s_ff, r_ff,
):
    b = lax.axis_index("batch")
    gy = lax.axis_index("gy")
    gx = lax.axis_index("gx")
    core = lax.rem(b, 2)
    bz = b // 2
    slot = gx * 4 + gy

    def group(p):
        return (b, lax.rem(p, 4), p // 4)

    def batch(p):
        return (p * 2 + core, gy, gx)

    partner = (b + 1 - 2 * core, gy, gx)

    mark("greet")
    loads = [
        pltpu.make_async_copy(h, v, s_in.at[i])
        for i, (h, v) in enumerate((
            (gf_h, gf), (gc_h, gc), (xf_h, xf), (xc_h, xc4), (dyc_h, dyc4), (wqkv_h, wqkv), (wout_h, wout),
            (dyf_h, dyf), (cw_h, cw), (cwo_h, cwo),
        ))
    ]
    for c in loads:
        c.start()
    barrier = pltpu.get_barrier_semaphore()

    def greet(i, carry):
        pl.semaphore_signal(barrier, inc=1, device_id=group(lax.rem(slot + i, 16)), device_id_type=MESH)
        pl.semaphore_signal(barrier, inc=1, device_id=batch(lax.rem(bz + i, 16)), device_id_type=MESH)
        return carry

    lax.fori_loop(1, 16, greet, 0)
    pl.semaphore_signal(barrier, inc=1, device_id=partner, device_id_type=MESH)

    mark("norms")
    step_value = t_ref[0].astype(F32)
    for c in loads[0:3]:
        c.wait()
    ff[...] = time_gain(gf[...], step_value)
    fc[...] = time_gain(gc[...], step_value)

    xff = xf[...].astype(F32)
    inv_f = lax.rsqrt(jnp.mean(xff * xff, axis=-1, keepdims=True) + eps)
    normf = xff * inv_f * ff[...]
    normed = normf.astype(BF16)
    nrm[0:256, :] = normed
    norm3 = normf.reshape(8, 32, 256)
    edge[0, :, :] = norm3[:, 0:8, :].reshape(64, 256).astype(BF16)
    edge[1, :, :] = norm3[:, 24:32, :].reshape(64, 256).astype(BF16)

    for c in loads[3:5]:
        c.wait()
    for r in range(4):
        xc[4 * r:4 * r + 4, :] = xc4[r].astype(F32)
    xcf = xc[...]
    inv_c = lax.rsqrt(jnp.mean(xcf * xcf, axis=-1, keepdims=True) + eps)
    ag[slot, 0:16, :] = (xcf * inv_c * fc[...]).astype(BF16)
    ag[slot, 16:32, :] = jnp.concatenate([dyc4[r].astype(F32) for r in range(4)], axis=0).astype(BF16)

    mark("barwait")
    pl.semaphore_wait(barrier, 31)

    mark("send0")
    src = {
        LEFT: edge.at[1], RIGHT: edge.at[0],
        TOP: nrm.at[pl.ds(160, 96)], BOTTOM: nrm.at[pl.ds(0, 96)],
        TL: edge.at[1, pl.ds(32, 32)], TR: edge.at[0, pl.ds(32, 32)],
        BL: edge.at[1, pl.ds(0, 32)], BR: edge.at[0, pl.ds(0, 32)],
    }

    def toward(step):
        return (b, lax.rem(gy + step[0] + 4, 4), lax.rem(gx + step[1] + 4, 4))

    def size(s):
        return SEGMENTS[s][1] * SEGMENTS[s][2]

    halo = []
    for s in range(1, 9):
        dy, dx = FROM[s]
        halo.append(rcopy(src[s], nrm.at[pl.ds(SEGMENTS[s][0], size(s))], s_h.at[s - 1], r_h.at[s - 1],
                          toward((-dy, -dx))))

    up, down, opp = lax.rem(gy + 1, 4), lax.rem(gy + 3, 4), lax.rem(gy + 2, 4)
    right, left, far = lax.rem(gx + 1, 4), lax.rem(gx + 3, 4), lax.rem(gx + 2, 4)
    to_up, to_down = (b, up, gx), (b, down, gx)
    to_right, to_left = (b, gy, right), (b, gy, left)
    sends = []

    def ag_send(g, x, part, device):
        sl = x * 4 + g
        block = ag.at[sl] if part is None else ag.at[sl, pl.ds(16 * part, 16)]
        c = rcopy(block, block, s_ag.at[len(sends)], r_ag.at[sl, part or 0], device)
        c.start()
        sends.append(c)

    def ag_wait(g, x, part=None):
        sl = x * 4 + g
        block = ag.at[sl] if part is None else ag.at[sl, pl.ds(16 * part, 16)]
        rcopy(block, block, s_ag.at[0], r_ag.at[sl, part or 0], to_up).wait_recv()

    for s in (TL, TR, BL, BR, TOP, BOTTOM, LEFT, RIGHT):
        halo[s - 1].start()
    ag_send(gy, gx, None, to_up)
    ag_send(gy, gx, None, to_down)
    ag_send(gy, gx, None, to_right)
    ag_send(gy, gx, None, to_left)

    mark("qmask")
    for c in loads[5:8]:
        c.wait()
    kv[0:256, :] = nn(normed, wqkv[:, 256:768]).astype(BF16)
    q = nn(normed, wqkv[:, 0:256])
    upst = nt(dyf[...], wout[...])
    lane = lax.broadcasted_iota(jnp.int32, (256, 256), 1) // HD
    for h in range(H_F):
        qm[h * 256:(h + 1) * 256, :] = jnp.where(lane == h, q, 0.0).astype(BF16)
        um[h * 256:(h + 1) * 256, :] = jnp.where(lane == h, upst, 0.0).astype(BF16)
    ok_side = {OWN: None, LEFT: gx > 0, RIGHT: gx < 3, TOP: gy > 0, BOTTOM: gy < 3,
               TL: (gx > 0) & (gy > 0), TR: (gx < 3) & (gy > 0),
               BL: (gx > 0) & (gy < 3), BR: (gx < 3) & (gy < 3)}
    for s, (first, rows, cols, row0, col0) in enumerate(SEGMENTS):
        n = rows * cols
        key = lax.broadcasted_iota(jnp.int32, (n, 256), 0)
        query = lax.broadcasted_iota(jnp.int32, (n, 256), 1)
        dr = key // cols + row0 - query // 32
        dc = lax.rem(key, cols) + col0 - lax.rem(query, 32)
        ok = (dr >= -RAD) & (dr <= RAD) & (dc >= -RAD) & (dc <= RAD)
        floor = jnp.where(ok, 0.0, -1e30).astype(F32)
        if ok_side[s] is not None:
            floor = jnp.minimum(floor, jnp.where(ok_side[s], 0.0, -1e30).astype(F32))
        bias[first:first + n, :] = floor

    def relay_near():
        ag_wait(gy, left)
        ag_send(gy, left, 0, to_right)
        ag_wait(gy, right)
        ag_send(gy, right, 1, to_left)
        ag_wait(down, gx)
        ag_send(down, gx, 0, to_up)
        ag_send(down, gx, None, to_right)
        ag_send(down, gx, None, to_left)
        ag_wait(up, gx)
        ag_send(up, gx, 1, to_down)
        ag_send(up, gx, None, to_right)
        ag_send(up, gx, None, to_left)

    def relay_opposite():
        ag_wait(opp, gx, 0)
        ag_wait(opp, gx, 1)
        ag_send(opp, gx, None, to_right)
        ag_send(opp, gx, None, to_left)

    def relay_side():
        for g in (down, up):
            ag_wait(g, left)
            ag_send(g, left, 0, to_right)
            ag_wait(g, right)
            ag_send(g, right, 1, to_left)

    def relay_last():
        ag_wait(opp, left)
        ag_send(opp, left, 0, to_right)
        ag_wait(opp, right)
        ag_send(opp, right, 1, to_left)

    mark("halowait")
    for c in halo:
        c.wait_recv()

    mark("transp")
    kv[256:KEYS, :] = nn(nrm[256:KEYS, :], wqkv[:, 256:768]).astype(BF16)
    kt[...] = kv[:, 0:256].T
    vt[...] = kv[:, 256:512].T

    def head(h):
        rows = slice(h * 64, (h + 1) * 64)
        heads = slice(h * 256, (h + 1) * 256)
        s = nt(kv[:, 0:256], qm[heads, :]) * scale + bias[...]
        top = jnp.max(s, axis=0, keepdims=True)
        e = jnp.exp(s - top)
        p = e * (1.0 / jnp.sum(e, axis=0, keepdims=True))
        w = p.astype(BF16)
        wall[:, heads] = w
        dp = nt(kv[:, 256:512], um[heads, :])
        delta = jnp.sum(p * dp, axis=0, keepdims=True)
        slope = (p * (dp - delta)).astype(BF16)
        sall[:, heads] = slope
        att[rows, :] = nn(vt[rows, :], w).astype(BF16)
        dqt[rows, :] = nn(kt[rows, :], slope) * scale

    mark("head01")
    head(0)
    head(1)
    mark("relaynear")
    relay_near()
    mark("head23")
    head(2)
    head(3)

    mark("finegrad")
    nt_all[...] = nrm[...].T
    dq = dqt[...].T.astype(BF16)
    dk = (nn(sall[...], qm[...]) * scale).astype(BF16)
    dv = nn(wall[...], um[...]).astype(BF16)
    parts = (
        (nn(nt_all[:, 0:256], dq), nn(nt_all[...], dk)),
        (nn(nt_all[...], dv), nn(att[...], dyf[...])),
    )
    for half in range(2):
        for i in range(2):
            fg[half, :, 256 * i:256 * (i + 1)] = parts[half][i]
            fgb[half, :, 256 * i:256 * (i + 1)] = parts[half][i].astype(BF16)
    fcc = rcopy(fgb.at[1 - core], fgp, s_fc.at[0], r_fc.at[0], partner)
    fcc.start()

    mark("gsend")
    gsend[...] = (nt(dk[256:KEYS], wqkv[:, 256:512]) + nt(dv[256:KEYS], wqkv[:, 512:768])).astype(BF16)
    ghalo = []
    for s in range(1, 9):
        dy, dx = FROM[s]
        o = BACK[s]
        c = rcopy(gsend.at[pl.ds(SEGMENTS[s][0] - 256, size(s))],
                  grecv.at[pl.ds(SEGMENTS[o][0] - 256, size(o))],
                  s_g.at[s - 1], r_g.at[s - 1], toward((dy, dx)))
        c.start()
        ghalo.append(c)
    dn[...] = (
        nt(dq, wqkv[:, 0:256]) + nt(dk[0:256], wqkv[:, 256:512]) + nt(dv[0:256], wqkv[:, 512:768])
    ).reshape(8, 32, 256)

    def spread(source, dest, ssem, rsem, me, device, each):
        def body(i, carry):
            p = lax.rem(me + i, 16)
            rcopy(source.at[p] if each else source, dest.at[me], ssem.at[i], rsem.at[me], device(p)).start()
            return carry
        lax.fori_loop(1, 16, body, 0)

    def collect(source, dest, ssem, rsem, me, device, each, forward=None):
        if forward is not None:
            forward(me).start()

        def body(i, carry):
            p = lax.rem(me + i, 16)
            c = rcopy(source.at[p] if each else source, dest.at[p], ssem.at[i], rsem.at[p], device(p))
            c.wait_recv()
            if forward is not None:
                forward(p).start()
            c.wait_send()
            return carry
        lax.fori_loop(1, 16, body, 0)

    def to_partner(dest, ssem, rsem):
        return lambda p: rcopy(dest.at[core, p], dest.at[core, p], ssem.at[p], rsem.at[p], partner)

    def from_partner(dest, ssem, rsem):
        def body(p, carry):
            c = rcopy(dest.at[1 - core, p], dest.at[1 - core, p], ssem.at[p], rsem.at[p], partner)
            c.wait_recv()
            c.wait_send()
            return carry
        lax.fori_loop(0, 16, body, 0)

    def total(dest):
        acc = dest[0].astype(F32)
        for i in range(1, 16):
            acc = acc + dest[i].astype(F32)
        return acc

    mark("relayopp")
    relay_opposite()
    mark("fccwait")
    fcc.wait_recv()
    f16[...] = (fg[core] + fgp[...].astype(F32)).astype(BF16).reshape(16, 16, 512)
    f16r[slot] = f16[slot]
    spread(f16, f16r, s_f16, r_f16, slot, group, True)
    mark("relayside")
    relay_side()
    mark("relaylast")
    relay_last()

    mark("agwait")
    for g in range(4):
        ag_wait(g, far, 0)
        ag_wait(g, far, 1)
    for c in loads[8:10]:
        c.wait()
    mark("coarse")
    nall = ag[:, 0:16, :].reshape(256, D_C)
    call = ag[:, 16:32, :].reshape(256, D_C)
    proj = nt(cw[...], nall).astype(BF16)
    cqt, ckt, cvt = proj[0:64], proj[64:128], proj[128:192]
    cut = nt(cwo[...], call).astype(BF16)
    cs = tn(ckt, cqt) * scale
    ce = jnp.exp(cs - jnp.max(cs, axis=0, keepdims=True))
    cp = ce * (1.0 / jnp.sum(ce, axis=0, keepdims=True))
    cwt = cp.astype(BF16)
    cot = nn(cvt, cwt).astype(BF16)
    cdp = tn(cvt, cut)
    cdelta = jnp.sum(cp * cdp, axis=0, keepdims=True)
    cslope = (cp * (cdp - cdelta)).astype(BF16)
    cdt = jnp.concatenate(
        [nn(ckt, cslope) * scale, nt(cqt, cslope) * scale, nt(cut, cwt)], axis=0
    ).astype(BF16)
    mark("rs")
    rs_send[...] = tn(cdt, cw[...]).astype(BF16).reshape(4, 4, 16, D_C)
    rx = []
    for i in (1, 3, 2):
        x = lax.rem(gx + i, 4)
        c = rcopy(rs_send.at[x], rsx.at[i], s_rx.at[i], r_rx.at[i], (b, gy, x))
        c.start()
        rx.append(c)
    mark("cgrad")
    cgq = nn(cdt, nall)
    cgo = nn(cot, call)
    for half in range(2):
        lanes = slice(half * 512, (half + 1) * 512)
        cg[half, 0:192, :] = cgq[:, lanes]
        cg[half, 192:256, :] = cgo[:, lanes]
        cgb[half, 0:192, :] = cgq[:, lanes].astype(BF16)
        cgb[half, 192:256, :] = cgo[:, lanes].astype(BF16)
    cc = rcopy(cgb.at[1 - core], cgp, s_cc.at[0], r_cc.at[0], partner)
    cc.start()

    mark("f16wait")
    collect(f16, f16r, s_f16, r_f16, slot, group, True)
    fone[bz] = total(f16r).astype(BF16)
    spread(fone.at[bz], fone, s_f1, r_f1, bz, batch, False)

    mark("ccwait")
    cc.wait_recv()
    c16[...] = (cg[core] + cgp[...].astype(F32)).astype(BF16).reshape(16, 16, 512)
    c16r[bz] = c16[bz]
    spread(c16, c16r, s_c16, r_c16, bz, batch, True)

    mark("rsx")
    acc = rs_send[gx].astype(F32)
    for i, c in zip((1, 3, 2), rx):
        c.wait_recv()
        acc = acc + rsx[i].astype(F32)
    rsz_send[...] = acc.astype(BF16)
    rz = []
    for i in (1, 3, 2):
        g = lax.rem(gy + i, 4)
        c = rcopy(rsz_send.at[g], rsz.at[i], s_rz.at[i], r_rz.at[i], (b, g, gx))
        c.start()
        rz.append(c)

    mark("ghalowait")
    for c in ghalo:
        c.wait_recv()

    def owed(s):
        first, rows, cols = SEGMENTS[s][:3]
        return grecv[first - 256:first - 256 + rows * cols, :].astype(F32).reshape(rows, cols, 256)

    mark("dxf")
    dn[:, 0:8, :] += owed(LEFT)
    dn[:, 24:32, :] += owed(RIGHT)
    dn[0:3, :, :] += owed(TOP)
    dn[5:8, :, :] += owed(BOTTOM)
    dn[0:4, 0:8, :] += owed(TL)
    dn[0:4, 24:32, :] += owed(TR)
    dn[4:8, 0:8, :] += owed(BL)
    dn[4:8, 24:32, :] += owed(BR)
    xff = xf[...].astype(F32)
    inv_f = lax.rsqrt(jnp.mean(xff * xff, axis=-1, keepdims=True) + eps)
    dxf[...] = norm_backward(xff, inv_f, ff[...], dn[...].reshape(256, 256))

    mark("c16wait")
    collect(c16, c16r, s_c16, r_c16, bz, batch, True)
    cmine = cfin.at[core, bz]
    cmine[...] = total(c16r).astype(BF16)
    spread(cmine, cfin.at[core], s_cag, r_cag, bz, batch, False)

    mark("fonewait")
    collect(fone.at[bz], fone, s_f1, r_f1, bz, batch, False)
    fmine = ffin.at[core, slot]
    fmine[...] = total(fone).astype(BF16)
    spread(fmine, ffin.at[core], s_fag, r_fag, slot, group, False)

    mark("rszwait")
    dnc = rsz_send[gy].astype(F32)
    for i, c in zip((1, 3, 2), rz):
        c.wait_recv()
        dnc = dnc + rsz[i].astype(F32)
    xcf = xc[...]
    inv_c = lax.rsqrt(jnp.mean(xcf * xcf, axis=-1, keepdims=True) + eps)
    dxcv = norm_backward(xcf, inv_c, fc[...], dnc)
    for r in range(4):
        dxc[r] = dxcv[4 * r:4 * r + 4]

    mark("cagwait")
    collect(cmine, cfin.at[core], s_cag, r_cag, bz, batch, False, to_partner(cfin, s_cf, r_cf))
    mark("cfwait")
    from_partner(cfin, s_cf, r_cf)
    for half in range(2):
        lanes = slice(half * 512, (half + 1) * 512)
        done = cfin[half].reshape(256, 512)
        gcq[:, lanes] = done[0:192]
        gco[:, lanes] = done[192:256]

    mark("fagwait")
    collect(fmine, ffin.at[core], s_fag, r_fag, slot, group, False, to_partner(ffin, s_ff, r_ff))
    mark("ffwait")
    from_partner(ffin, s_ff, r_ff)
    gfq[:, 0:512] = ffin[0].reshape(256, 512)
    done = ffin[1].reshape(256, 512)
    gfq[:, 512:768] = done[:, 0:256]
    gfo[...] = done[:, 256:512]

    mark("sendwait")
    for c in sends + halo + ghalo + rx + rz + [cc, fcc]:
        c.wait_send()
    mark(None)


def writer(*refs):
    sems = refs[12]
    copies = [pltpu.make_async_copy(refs[i], refs[6 + i], sems.at[i]) for i in range(6)]
    for c in copies:
        c.start()
    for c in copies:
        c.wait()


def local(x_fine, dy_fine, x_coarse, dy_coarse, timestep, fine_gain, coarse_gain,
          fine_qkv, fine_out, coarse_qkv, coarse_out):
    vm = pl.BlockSpec(memory_space=pltpu.VMEM)
    hbm = pl.BlockSpec(memory_space=pltpu.HBM)
    dma = pltpu.SemaphoreType.DMA
    V = pltpu.VMEM
    outs = (
        jax.ShapeDtypeStruct((256, 256), BF16),
        jax.ShapeDtypeStruct((4, 4, D_C), BF16),
        jax.ShapeDtypeStruct((256, 768), BF16),
        jax.ShapeDtypeStruct((256, 256), BF16),
        jax.ShapeDtypeStruct((192, D_C), BF16),
        jax.ShapeDtypeStruct((64, D_C), BF16),
    )
    scratch = [
        V((256, 256), BF16), V((256, 256), BF16), V((4, 4, D_C), BF16), V((4, 4, D_C), BF16),
        V((1, 256), F32), V((1, D_C), F32), V((256, 768), BF16), V((256, 256), BF16),
        V((192, D_C), BF16), V((64, D_C), BF16), V((16, D_C), F32), V((1, 256), F32), V((1, D_C), F32),
        V((16, 32, D_C), BF16), V((KEYS, 256), BF16), V((KEYS, 512), BF16), V((2, 64, 256), BF16),
        V((KEYS, 256), F32), V((1024, 256), BF16), V((1024, 256), BF16),
        V((256, KEYS), BF16), V((256, KEYS), BF16), V((256, KEYS), BF16),
        V((KEYS, 1024), BF16), V((KEYS, 1024), BF16),
        V((256, 256), BF16), V((256, 256), F32), V((8, 32, 256), F32),
        V((HALO, 256), BF16), V((HALO, 256), BF16),
        V((4, 4, 16, D_C), BF16), V((4, 4, 16, D_C), BF16), V((4, 16, D_C), BF16), V((4, 16, D_C), BF16),
        V((2, 256, 512), F32), V((2, 256, 512), BF16), V((256, 512), BF16),
        V((16, 16, 512), BF16), V((16, 16, 512), BF16), V((2, 16, 16, 512), BF16),
        V((2, 256, 512), F32), V((2, 256, 512), BF16), V((256, 512), BF16),
        V((16, 16, 512), BF16), V((16, 16, 512), BF16), V((16, 16, 512), BF16), V((2, 16, 16, 512), BF16),
        dma((10,)), dma((24,)), dma((16, 2)), dma((8,)), dma((8,)), dma((8,)), dma((8,)),
        dma((4,)), dma((4,)), dma((4,)), dma((4,)),
        dma((2,)), dma((2,)), dma((16,)), dma((16,)), dma((16,)), dma((16,)), dma((16,)), dma((16,)),
        dma((2,)), dma((2,)), dma((16,)), dma((16,)), dma((16,)), dma((16,)), dma((16,)), dma((16,)),
        dma((16,)), dma((16,)),
    ]
    results = pl.pallas_call(
        kernel,
        out_shape=outs,
        in_specs=[pl.BlockSpec(memory_space=pltpu.SMEM)] + [hbm] * 10,
        out_specs=[vm] * 6,
        scratch_shapes=scratch,
        compiler_params=pltpu.CompilerParams(
            collective_id=0, has_side_effects=True, vmem_limit_bytes=50 * 1024 * 1024
        ),
    )(timestep, *[
        pltpu.with_memory_space_constraint(a, pltpu.HBM) for a in (
            x_fine.reshape(256, D_F), dy_fine.reshape(256, D_F),
            x_coarse.reshape(4, 4, D_C), dy_coarse.reshape(4, 4, D_C),
            fine_gain[None], coarse_gain[None],
            fine_qkv, fine_out, coarse_qkv.reshape(192, D_C), coarse_out,
        )
    ])
    dxf, dxc, gfq, gfo, gcq, gco = pl.pallas_call(
        writer,
        out_shape=tuple(pltpu.HBM(o.shape, o.dtype) for o in outs),
        in_specs=[vm] * 6,
        out_specs=[hbm] * 6,
        scratch_shapes=[dma((6,))],
    )(*[pltpu.with_memory_space_constraint(r, pltpu.VMEM) for r in results])
    return (
        dxf.reshape(x_fine.shape),
        dxc.reshape(x_coarse.shape),
        gfq,
        gfo,
        gcq.reshape(coarse_qkv.shape),
        gco,
    )


def solution(mesh):
    tile = P("batch", "gy", "gx", None)
    heads = P(None, ("gy", "gx"), None)
    rows = P(("gy", "gx"), None)
    return jax.shard_map(
        local,
        mesh=mesh,
        in_specs=(tile, tile, tile, tile, P("batch"), P(), P(), P(), P(), heads, rows),
        out_specs=(tile, tile, P(), P(), heads, rows),
        check_vma=False,
    )
```

```python
import math

import jax
import jax.numpy as jnp
from jax import lax
from jax.experimental import pallas as pl
from jax.experimental.pallas import tpu as pltpu
from jax.sharding import PartitionSpec as P

D_F = 256
H_F = 4
D_C = 1024
HD = 64
RAD = 3
F32 = jnp.float32
BF16 = jnp.bfloat16
MESH = pl.DeviceIdType.MESH

eps = 1e-06
log_span = math.log(1000.0)
scale = 1.0 / math.sqrt(HD)

OWN, LEFT, RIGHT, TOP, BOTTOM, TL, TR, BL, BR = range(9)
SEGMENTS = (
    (0, 8, 32, 0, 0),
    (256, 8, 4, 0, -4),
    (288, 8, 4, 0, 32),
    (320, 3, 32, -3, 0),
    (416, 3, 32, 8, 0),
    (512, 4, 4, -4, -4),
    (528, 4, 4, -4, 32),
    (544, 4, 4, 8, -4),
    (560, 4, 4, 8, 32),
)
KEYS = 576
HALO = KEYS - 256
FROM = {LEFT: (0, -1), RIGHT: (0, 1), TOP: (-1, 0), BOTTOM: (1, 0),
        TL: (-1, -1), TR: (-1, 1), BL: (1, -1), BR: (1, 1)}
BACK = {LEFT: RIGHT, RIGHT: LEFT, TOP: BOTTOM, BOTTOM: TOP, TL: BR, BR: TL, TR: BL, BL: TR}


def nn(a, b):
    return lax.dot_general(a, b, (((1,), (0,)), ((), ())), preferred_element_type=F32)


def nt(a, b):
    return lax.dot_general(a, b, (((1,), (1,)), ((), ())), preferred_element_type=F32)


def tn(a, b):
    return lax.dot_general(a, b, (((0,), (0,)), ((), ())), preferred_element_type=F32)


def mark(name):
    pass


def rcopy(src, dst, ssem, rsem, device):
    return pltpu.make_async_remote_copy(
        src_ref=src, dst_ref=dst, send_sem=ssem, recv_sem=rsem,
        device_id=device, device_id_type=MESH,
    )


def time_gain(gains, step_value):
    channels = gains.shape[1]
    place = lax.broadcasted_iota(jnp.int32, (8, channels), 1).astype(F32)
    frequency = jnp.exp(-log_span * place / channels)
    factor = jnp.cos(step_value * frequency)
    return gains * (1.0 + 0.5 * factor[0:1])


def norm_backward(floats, inverse, factor, upstream):
    scaled = upstream * factor
    middle = jnp.mean(floats * scaled, axis=-1, keepdims=True)
    return (inverse * scaled - floats * inverse * inverse * inverse * middle).astype(BF16)


def kernel(
    t_ref, xf_h, dyf_h, xc_h, dyc_h, gf_h, gc_h, wqkv_h, wout_h, cw_h, cwo_h,
    dxf, dxc, gfq, gfo, gcq, gco,
    xf, dyf, xc4, dyc4, gf, gc, wqkv, wout, cw, cwo, xc, ff, fc,
    ag, nrm, kv, edge32, edge, bias, qm, um, kt, vt, nt_all, wall, sall, att, dqt, dn, gsend, grecv,
    rs_send, rsx, rsz_send, rsz,
    cg, cgb, cgp, c16, c16r, cfin,
    fg, fgb, fgp, fxs, fxr, fzs, fzr, fyr, ffin,
    s_in, s_ag, r_ag, s_h, r_h, s_g, r_g, s_rx, r_rx, s_rz, r_rz,
    s_cc, r_cc, s_c16, r_c16, s_cag, r_cag, s_cf, r_cf,
    s_fc, r_fc, s_fx, r_fx, s_fz, r_fz, s_fy, r_fy, s_fzg, r_fzg, s_fxg, r_fxg, s_ff, r_ff,
):
    b = lax.axis_index("batch")
    gy = lax.axis_index("gy")
    gx = lax.axis_index("gx")
    core = lax.rem(b, 2)
    bz = b // 2
    slot = gx * 4 + gy

    def group(p):
        return (b, lax.rem(p, 4), p // 4)

    def batch(p):
        return (p * 2 + core, gy, gx)

    partner = (b + 1 - 2 * core, gy, gx)

    zlo = b // 16
    yy = lax.rem(bz, 8)
    zz = gy * 2 + zlo

    def along_z(p):
        return (lax.rem(p, 2) * 16 + yy * 2 + core, p // 2, gx)

    def along_y(p):
        return (zlo * 16 + p * 2 + core, gy, gx)

    mark("greet")
    loads = [
        pltpu.make_async_copy(h, v, s_in.at[i])
        for i, (h, v) in enumerate((
            (gf_h, gf), (gc_h, gc), (xf_h, xf), (xc_h, xc4), (dyc_h, dyc4), (wqkv_h, wqkv), (wout_h, wout),
            (dyf_h, dyf), (cw_h, cw), (cwo_h, cwo),
        ))
    ]
    for c in loads:
        c.start()
    barrier = pltpu.get_barrier_semaphore()

    def greet(i, carry):
        pl.semaphore_signal(barrier, inc=1, device_id=group(lax.rem(slot + i, 16)), device_id_type=MESH)
        pl.semaphore_signal(barrier, inc=1, device_id=batch(lax.rem(bz + i, 16)), device_id_type=MESH)
        return carry

    lax.fori_loop(1, 16, greet, 0)
    pl.semaphore_signal(barrier, inc=1, device_id=partner, device_id_type=MESH)
    for i in (1, 2, 3):
        other = along_z(lax.rem(gy + i, 4) * 2 + 1 - zlo)
        pl.semaphore_signal(barrier, inc=1, device_id=other, device_id_type=MESH)

    mark("norms")
    step_value = t_ref[0].astype(F32)
    for c in loads[0:3]:
        c.wait()
    ff[...] = time_gain(gf[...], step_value)
    fc[...] = time_gain(gc[...], step_value)

    xff = xf[...].astype(F32)
    inv_f = lax.rsqrt(jnp.mean(xff * xff, axis=-1, keepdims=True) + eps)
    normf = xff * inv_f * ff[...]
    normed = normf.astype(BF16)
    nrm[0:256, :] = normed
    norm3 = normf.reshape(8, 32, 256)
    for r in range(8):
        edge32[0, 4 * r:4 * r + 4, :] = norm3[r, 0:4, :]
        edge32[1, 4 * r:4 * r + 4, :] = norm3[r, 28:32, :]
    edge[...] = edge32[...].astype(BF16)

    for c in loads[3:5]:
        c.wait()
    for r in range(4):
        xc[4 * r:4 * r + 4, :] = xc4[r].astype(F32)
    xcf = xc[...]
    inv_c = lax.rsqrt(jnp.mean(xcf * xcf, axis=-1, keepdims=True) + eps)
    ag[slot, 0:16, :] = (xcf * inv_c * fc[...]).astype(BF16)
    ag[slot, 16:32, :] = jnp.concatenate([dyc4[r].astype(F32) for r in range(4)], axis=0).astype(BF16)

    mark("barwait")
    pl.semaphore_wait(barrier, 34)

    mark("send0")
    src = {
        LEFT: edge.at[1], RIGHT: edge.at[0],
        TOP: nrm.at[pl.ds(160, 96)], BOTTOM: nrm.at[pl.ds(0, 96)],
        TL: edge.at[1, pl.ds(16, 16)], TR: edge.at[0, pl.ds(16, 16)],
        BL: edge.at[1, pl.ds(0, 16)], BR: edge.at[0, pl.ds(0, 16)],
    }

    def toward(step):
        return (b, lax.rem(gy + step[0] + 4, 4), lax.rem(gx + step[1] + 4, 4))

    def size(s):
        return SEGMENTS[s][1] * SEGMENTS[s][2]

    halo = []
    for s in range(1, 9):
        dy, dx = FROM[s]
        halo.append(rcopy(src[s], nrm.at[pl.ds(SEGMENTS[s][0], size(s))], s_h.at[s - 1], r_h.at[s - 1],
                          toward((-dy, -dx))))

    up, down, opp = lax.rem(gy + 1, 4), lax.rem(gy + 3, 4), lax.rem(gy + 2, 4)
    right, left, far = lax.rem(gx + 1, 4), lax.rem(gx + 3, 4), lax.rem(gx + 2, 4)
    sends = []

    def ag_copy(g, x, part, device):
        sl = x * 4 + g
        block = ag.at[sl] if part is None else ag.at[sl, pl.ds(16 * part, 16)]
        return rcopy(block, block, s_ag.at[len(sends)], r_ag.at[sl, part or 0], device)

    def ag_send(g, x, device, part=None):
        c = ag_copy(g, x, part, device)
        c.start()
        sends.append(c)

    def ag_wait(g, x, part=None):
        ag_copy(g, x, part, partner).wait_recv()

    for g in (up, down):
        ag_send(gy, gx, (b, g, gx))
    for x in (far, right, left):
        ag_send(gy, gx, (b, gy, x))
    for s in (TL, TR, BL, BR, TOP, BOTTOM, LEFT, RIGHT):
        halo[s - 1].start()

    mark("qmask")
    for c in loads[5:8]:
        c.wait()
    kv[0:256, :] = nn(normed, wqkv[:, 256:768]).astype(BF16)
    q = nn(normed, wqkv[:, 0:256])
    upst = nt(dyf[...], wout[...])
    lane = lax.broadcasted_iota(jnp.int32, (256, 256), 1) // HD
    for h in range(H_F):
        qm[h * 256:(h + 1) * 256, :] = jnp.where(lane == h, q, 0.0).astype(BF16)
        um[h * 256:(h + 1) * 256, :] = jnp.where(lane == h, upst, 0.0).astype(BF16)
    ok_side = {OWN: None, LEFT: gx > 0, RIGHT: gx < 3, TOP: gy > 0, BOTTOM: gy < 3,
               TL: (gx > 0) & (gy > 0), TR: (gx < 3) & (gy > 0),
               BL: (gx > 0) & (gy < 3), BR: (gx < 3) & (gy < 3)}
    for s, (first, rows, cols, row0, col0) in enumerate(SEGMENTS):
        n = rows * cols
        key = lax.broadcasted_iota(jnp.int32, (n, 256), 0)
        query = lax.broadcasted_iota(jnp.int32, (n, 256), 1)
        dr = key // cols + row0 - query // 32
        dc = lax.rem(key, cols) + col0 - lax.rem(query, 32)
        ok = (dr >= -RAD) & (dr <= RAD) & (dc >= -RAD) & (dc <= RAD)
        floor = jnp.where(ok, 0.0, -1e30).astype(F32)
        if ok_side[s] is not None:
            floor = jnp.minimum(floor, jnp.where(ok_side[s], 0.0, -1e30).astype(F32))
        bias[first:first + n, :] = floor

    mark("forward")
    for g, part, device in ((down, 0, (b, up, gx)), (up, 1, (b, down, gx))):
        ag_wait(g, gx)
        ag_send(g, gx, device, part)
        for x in (far, right, left):
            ag_send(g, gx, (b, gy, x))

    mark("halowait")
    for c in halo:
        c.wait_recv()

    mark("transp")
    kv[256:KEYS, :] = nn(nrm[256:KEYS, :], wqkv[:, 256:768]).astype(BF16)
    kt[...] = kv[:, 0:256].T
    vt[...] = kv[:, 256:512].T

    def head(h):
        rows = slice(h * 64, (h + 1) * 64)
        heads = slice(h * 256, (h + 1) * 256)
        s = nt(kv[:, 0:256], qm[heads, :]) * scale + bias[...]
        top = jnp.max(s, axis=0, keepdims=True)
        e = jnp.exp(s - top)
        p = e * (1.0 / jnp.sum(e, axis=0, keepdims=True))
        w = p.astype(BF16)
        wall[:, heads] = w
        dp = nt(kv[:, 256:512], um[heads, :])
        delta = jnp.sum(p * dp, axis=0, keepdims=True)
        slope = (p * (dp - delta)).astype(BF16)
        sall[:, heads] = slope
        att[rows, :] = nn(vt[rows, :], w).astype(BF16)
        dqt[rows, :] = nn(kt[rows, :], slope) * scale

    mark("head01")
    head(0)
    head(1)
    mark("forward2")
    ag_wait(opp, gx, 0)
    ag_wait(opp, gx, 1)
    for x in (far, right, left):
        ag_send(opp, gx, (b, gy, x))
    mark("head23")
    head(2)
    head(3)

    mark("finegrad")
    nt_all[...] = nrm[...].T
    dq = dqt[...].T.astype(BF16)
    dk = (nn(sall[...], qm[...]) * scale).astype(BF16)
    dv = nn(wall[...], um[...]).astype(BF16)
    parts = (
        (nn(nt_all[:, 0:256], dq), nn(nt_all[...], dk)),
        (nn(nt_all[...], dv), nn(att[...], dyf[...])),
    )
    for half in range(2):
        for i in range(2):
            fg[half, :, 256 * i:256 * (i + 1)] = parts[half][i]
            fgb[half, :, 256 * i:256 * (i + 1)] = parts[half][i].astype(BF16)
    fcc = rcopy(fgb.at[1 - core], fgp, s_fc.at[0], r_fc.at[0], partner)
    fcc.start()

    mark("gsend")
    gsend[...] = (nt(dk[256:KEYS], wqkv[:, 256:512]) + nt(dv[256:KEYS], wqkv[:, 512:768])).astype(BF16)
    ghalo = []
    for s in range(1, 9):
        dy, dx = FROM[s]
        o = BACK[s]
        c = rcopy(gsend.at[pl.ds(SEGMENTS[s][0] - 256, size(s))],
                  grecv.at[pl.ds(SEGMENTS[o][0] - 256, size(o))],
                  s_g.at[s - 1], r_g.at[s - 1], toward((dy, dx)))
        c.start()
        ghalo.append(c)
    dn[...] = (
        nt(dq, wqkv[:, 0:256]) + nt(dk[0:256], wqkv[:, 256:512]) + nt(dv[0:256], wqkv[:, 512:768])
    ).reshape(8, 32, 256)

    def spread(source, dest, ssem, rsem, me, device, each, n=16):
        def body(i, carry):
            p = lax.rem(me + i, n)
            rcopy(source.at[p] if each else source, dest.at[me], ssem.at[i], rsem.at[me], device(p)).start()
            return carry
        lax.fori_loop(1, n, body, 0)

    def collect(source, dest, ssem, rsem, me, device, each, forward=None, n=16):
        if forward is not None:
            forward(me).start()

        def body(i, carry):
            p = lax.rem(me + i, n)
            c = rcopy(source.at[p] if each else source, dest.at[p], ssem.at[i], rsem.at[p], device(p))
            c.wait_recv()
            if forward is not None:
                forward(p).start()
            c.wait_send()
            return carry
        lax.fori_loop(1, n, body, 0)

    def to_partner(dest, ssem, rsem):
        return lambda p: rcopy(dest.at[core, p], dest.at[core, p], ssem.at[p], rsem.at[p], partner)

    def from_partner(dest, ssem, rsem, n=16):
        def body(p, carry):
            c = rcopy(dest.at[1 - core, p], dest.at[1 - core, p], ssem.at[p], rsem.at[p], partner)
            c.wait_recv()
            c.wait_send()
            return carry
        lax.fori_loop(0, n, body, 0)

    def total(dest, n=16):
        acc = dest[0].astype(F32)
        for i in range(1, n):
            acc = acc + dest[i].astype(F32)
        return acc

    mark("fccwait")
    fcc.wait_recv()
    fxs[...] = (fg[core] + fgp[...].astype(F32)).astype(BF16).reshape(4, 64, 512)
    fx = []
    for i in (1, 3, 2):
        x = lax.rem(gx + i, 4)
        c = rcopy(fxs.at[x], fxr.at[i], s_fx.at[i], r_fx.at[i], (b, gy, x))
        c.start()
        fx.append(c)
    mark("agwait")
    for g in (gy, down, up, opp):
        for x in (right, left, far):
            ag_wait(g, x)
    for c in loads[8:10]:
        c.wait()
    mark("coarse")
    nall = ag[:, 0:16, :].reshape(256, D_C)
    call = ag[:, 16:32, :].reshape(256, D_C)
    proj = nt(cw[...], nall).astype(BF16)
    cqt, ckt, cvt = proj[0:64], proj[64:128], proj[128:192]
    cut = nt(cwo[...], call).astype(BF16)
    cs = tn(ckt, cqt) * scale
    ce = jnp.exp(cs - jnp.max(cs, axis=0, keepdims=True))
    cp = ce * (1.0 / jnp.sum(ce, axis=0, keepdims=True))
    cwt = cp.astype(BF16)
    cot = nn(cvt, cwt).astype(BF16)
    cdp = tn(cvt, cut)
    cdelta = jnp.sum(cp * cdp, axis=0, keepdims=True)
    cslope = (cp * (cdp - cdelta)).astype(BF16)
    cdt = jnp.concatenate(
        [nn(ckt, cslope) * scale, nt(cqt, cslope) * scale, nt(cut, cwt)], axis=0
    ).astype(BF16)
    mark("rs")
    rs_send[...] = tn(cdt, cw[...]).astype(BF16).reshape(4, 4, 16, D_C)
    rx = []
    for i in (1, 3, 2):
        x = lax.rem(gx + i, 4)
        c = rcopy(rs_send.at[x], rsx.at[i], s_rx.at[i], r_rx.at[i], (b, gy, x))
        c.start()
        rx.append(c)
    mark("cgrad")
    cgq = nn(cdt, nall)
    cgo = nn(cot, call)
    for half in range(2):
        lanes = slice(half * 512, (half + 1) * 512)
        cg[half, 0:192, :] = cgq[:, lanes]
        cg[half, 192:256, :] = cgo[:, lanes]
        cgb[half, 0:192, :] = cgq[:, lanes].astype(BF16)
        cgb[half, 192:256, :] = cgo[:, lanes].astype(BF16)
    cc = rcopy(cgb.at[1 - core], cgp, s_cc.at[0], r_cc.at[0], partner)
    cc.start()

    mark("fxwait")
    acc = fxs[gx].astype(F32)
    for i, c in zip((1, 3, 2), fx):
        c.wait_recv()
        acc = acc + fxr[i].astype(F32)
    for j in range(2):
        fzs[4 * j:4 * j + 4] = acc[:, 256 * j:256 * (j + 1)].astype(BF16).reshape(4, 16, 256)
    fzr[zz] = fzs[zz]
    spread(fzs, fzr, s_fz, r_fz, zz, along_z, True, n=8)

    mark("ccwait")
    cc.wait_recv()
    c16[...] = (cg[core] + cgp[...].astype(F32)).astype(BF16).reshape(16, 16, 512)
    c16r[bz] = c16[bz]
    spread(c16, c16r, s_c16, r_c16, bz, batch, True)

    mark("fzwait")
    collect(fzs, fzr, s_fz, r_fz, zz, along_z, True, n=8)
    fyr[yy] = total(fzr, 8).astype(BF16)
    spread(fyr.at[yy], fyr, s_fy, r_fy, yy, along_y, False, n=8)

    mark("rsx")
    acc = rs_send[gx].astype(F32)
    for i, c in zip((1, 3, 2), rx):
        c.wait_recv()
        acc = acc + rsx[i].astype(F32)
    rsz_send[...] = acc.astype(BF16)
    rz = []
    for i in (1, 3, 2):
        g = lax.rem(gy + i, 4)
        c = rcopy(rsz_send.at[g], rsz.at[i], s_rz.at[i], r_rz.at[i], (b, g, gx))
        c.start()
        rz.append(c)

    mark("ghalowait")
    for c in ghalo:
        c.wait_recv()

    def owed(s):
        first, rows, cols = SEGMENTS[s][:3]
        return grecv[first - 256:first - 256 + rows * cols, :].astype(F32).reshape(rows, cols, 256)

    mark("dxf")
    dn[0:3, :, :] += owed(TOP)
    dn[5:8, :, :] += owed(BOTTOM)
    for s, row0, col0 in ((LEFT, 0, 0), (RIGHT, 0, 28), (TL, 0, 0), (TR, 0, 28), (BL, 4, 0), (BR, 4, 28)):
        share = owed(s)
        for r in range(SEGMENTS[s][1]):
            dn[row0 + r, col0:col0 + 4, :] += share[r]
    xff = xf[...].astype(F32)
    inv_f = lax.rsqrt(jnp.mean(xff * xff, axis=-1, keepdims=True) + eps)
    dxf[...] = norm_backward(xff, inv_f, ff[...], dn[...].reshape(256, 256))

    mark("fywait")
    collect(fyr.at[yy], fyr, s_fy, r_fy, yy, along_y, False, n=8)
    fcol = ffin.at[core, gx]
    fmine = fcol.at[zz]
    fmine[...] = total(fyr, 8).astype(BF16)
    spread(fmine, fcol, s_fzg, r_fzg, zz, along_z, False, n=8)

    mark("c16wait")
    collect(c16, c16r, s_c16, r_c16, bz, batch, True)
    cmine = cfin.at[core, bz]
    cmine[...] = total(c16r).astype(BF16)
    spread(cmine, cfin.at[core], s_cag, r_cag, bz, batch, False)

    mark("rszwait")
    dnc = rsz_send[gy].astype(F32)
    for i, c in zip((1, 3, 2), rz):
        c.wait_recv()
        dnc = dnc + rsz[i].astype(F32)
    xcf = xc[...]
    inv_c = lax.rsqrt(jnp.mean(xcf * xcf, axis=-1, keepdims=True) + eps)
    dxcv = norm_backward(xcf, inv_c, fc[...], dnc)
    for r in range(4):
        dxc[r] = dxcv[4 * r:4 * r + 4]

    mark("fzgwait")
    collect(fmine, fcol, s_fzg, r_fzg, zz, along_z, False, n=8)
    spread(fcol, ffin.at[core], s_fxg, r_fxg, gx, lambda p: (b, gy, p), False, n=4)

    mark("cagwait")
    collect(cmine, cfin.at[core], s_cag, r_cag, bz, batch, False, to_partner(cfin, s_cf, r_cf))
    mark("cfwait")
    from_partner(cfin, s_cf, r_cf)
    for half in range(2):
        lanes = slice(half * 512, (half + 1) * 512)
        done = cfin[half].reshape(256, 512)
        gcq[:, lanes] = done[0:192]
        gco[:, lanes] = done[192:256]

    mark("fxgwait")
    collect(fcol, ffin.at[core], s_fxg, r_fxg, gx, lambda p: (b, gy, p), False, to_partner(ffin, s_ff, r_ff), n=4)
    mark("ffwait")
    from_partner(ffin, s_ff, r_ff, n=4)
    for x in range(4):
        rows = slice(64 * x, 64 * (x + 1))
        quarter = [ffin[half, x, 4 * j:4 * j + 4].reshape(64, 256) for half in range(2) for j in range(2)]
        for i in range(3):
            gfq[rows, 256 * i:256 * (i + 1)] = quarter[i]
        gfo[rows, :] = quarter[3]

    mark("sendwait")
    for c in sends + halo + ghalo + rx + rz + fx + [cc, fcc]:
        c.wait_send()
    mark(None)


def writer(*refs):
    sems = refs[12]
    copies = [pltpu.make_async_copy(refs[i], refs[6 + i], sems.at[i]) for i in range(6)]
    for c in copies:
        c.start()
    for c in copies:
        c.wait()


def local(x_fine, dy_fine, x_coarse, dy_coarse, timestep, fine_gain, coarse_gain,
          fine_qkv, fine_out, coarse_qkv, coarse_out):
    vm = pl.BlockSpec(memory_space=pltpu.VMEM)
    hbm = pl.BlockSpec(memory_space=pltpu.HBM)
    dma = pltpu.SemaphoreType.DMA
    V = pltpu.VMEM
    outs = (
        jax.ShapeDtypeStruct((256, 256), BF16),
        jax.ShapeDtypeStruct((4, 4, D_C), BF16),
        jax.ShapeDtypeStruct((256, 768), BF16),
        jax.ShapeDtypeStruct((256, 256), BF16),
        jax.ShapeDtypeStruct((192, D_C), BF16),
        jax.ShapeDtypeStruct((64, D_C), BF16),
    )
    scratch = [
        V((256, 256), BF16), V((256, 256), BF16), V((4, 4, D_C), BF16), V((4, 4, D_C), BF16),
        V((1, 256), F32), V((1, D_C), F32), V((256, 768), BF16), V((256, 256), BF16),
        V((192, D_C), BF16), V((64, D_C), BF16), V((16, D_C), F32), V((1, 256), F32), V((1, D_C), F32),
        V((16, 32, D_C), BF16), V((KEYS, 256), BF16), V((KEYS, 512), BF16), V((2, 32, 256), F32), V((2, 32, 256), BF16),
        V((KEYS, 256), F32), V((1024, 256), BF16), V((1024, 256), BF16),
        V((256, KEYS), BF16), V((256, KEYS), BF16), V((256, KEYS), BF16),
        V((KEYS, 1024), BF16), V((KEYS, 1024), BF16),
        V((256, 256), BF16), V((256, 256), F32), V((8, 32, 256), F32),
        V((HALO, 256), BF16), V((HALO, 256), BF16),
        V((4, 4, 16, D_C), BF16), V((4, 4, 16, D_C), BF16), V((4, 16, D_C), BF16), V((4, 16, D_C), BF16),
        V((2, 256, 512), F32), V((2, 256, 512), BF16), V((256, 512), BF16),
        V((16, 16, 512), BF16), V((16, 16, 512), BF16), V((2, 16, 16, 512), BF16),
        V((2, 256, 512), F32), V((2, 256, 512), BF16), V((256, 512), BF16),
        V((4, 64, 512), BF16), V((4, 64, 512), BF16), V((8, 16, 256), BF16), V((8, 16, 256), BF16),
        V((8, 16, 256), BF16), V((2, 4, 8, 16, 256), BF16),
        dma((10,)), dma((16,)), dma((16, 2)), dma((8,)), dma((8,)), dma((8,)), dma((8,)),
        dma((4,)), dma((4,)), dma((4,)), dma((4,)),
        dma((2,)), dma((2,)), dma((16,)), dma((16,)), dma((16,)), dma((16,)), dma((16,)), dma((16,)),
        dma((2,)), dma((2,)), dma((4,)), dma((4,)), dma((8,)), dma((8,)), dma((8,)), dma((8,)),
        dma((8,)), dma((8,)), dma((4,)), dma((4,)), dma((4,)), dma((4,)),
    ]
    results = pl.pallas_call(
        kernel,
        out_shape=outs,
        in_specs=[pl.BlockSpec(memory_space=pltpu.SMEM)] + [hbm] * 10,
        out_specs=[vm] * 6,
        scratch_shapes=scratch,
        compiler_params=pltpu.CompilerParams(
            collective_id=0, has_side_effects=True, vmem_limit_bytes=50 * 1024 * 1024
        ),
    )(timestep, *[
        pltpu.with_memory_space_constraint(a, pltpu.HBM) for a in (
            x_fine.reshape(256, D_F), dy_fine.reshape(256, D_F),
            x_coarse.reshape(4, 4, D_C), dy_coarse.reshape(4, 4, D_C),
            fine_gain[None], coarse_gain[None],
            fine_qkv, fine_out, coarse_qkv.reshape(192, D_C), coarse_out,
        )
    ])
    dxf, dxc, gfq, gfo, gcq, gco = pl.pallas_call(
        writer,
        out_shape=tuple(pltpu.HBM(o.shape, o.dtype) for o in outs),
        in_specs=[vm] * 6,
        out_specs=[hbm] * 6,
        scratch_shapes=[dma((6,))],
    )(*[pltpu.with_memory_space_constraint(r, pltpu.VMEM) for r in results])
    return (
        dxf.reshape(x_fine.shape),
        dxc.reshape(x_coarse.shape),
        gfq,
        gfo,
        gcq.reshape(coarse_qkv.shape),
        gco,
    )


def solution(mesh):
    tile = P("batch", "gy", "gx", None)
    heads = P(None, ("gy", "gx"), None)
    rows = P(("gy", "gx"), None)
    return jax.shard_map(
        local,
        mesh=mesh,
        in_specs=(tile, tile, tile, tile, P("batch"), P(), P(), P(), P(), heads, rows),
        out_specs=(tile, tile, P(), P(), heads, rows),
        check_vma=False,
    )
```

```python
import math

import jax
import jax.numpy as jnp
from jax import lax
from jax.experimental import pallas as pl
from jax.experimental.pallas import tpu as pltpu
from jax.sharding import PartitionSpec as P

D_F = 256
H_F = 4
D_C = 1024
HD = 64
RAD = 3
F32 = jnp.float32
BF16 = jnp.bfloat16
MESH = pl.DeviceIdType.MESH

eps = 1e-06
log_span = math.log(1000.0)
scale = 1.0 / math.sqrt(HD)

OWN, LEFT, RIGHT, TOP, BOTTOM, TL, TR, BL, BR = range(9)
SEGMENTS = (
    (0, 8, 32, 0, 0),
    (256, 8, 4, 0, -4),
    (288, 8, 4, 0, 32),
    (320, 3, 32, -3, 0),
    (416, 3, 32, 8, 0),
    (512, 4, 4, -4, -4),
    (528, 4, 4, -4, 32),
    (544, 4, 4, 8, -4),
    (560, 4, 4, 8, 32),
)
KEYS = 576
HALO = KEYS - 256
FROM = {LEFT: (0, -1), RIGHT: (0, 1), TOP: (-1, 0), BOTTOM: (1, 0),
        TL: (-1, -1), TR: (-1, 1), BL: (1, -1), BR: (1, 1)}
BACK = {LEFT: RIGHT, RIGHT: LEFT, TOP: BOTTOM, BOTTOM: TOP, TL: BR, BR: TL, TR: BL, BL: TR}


def nn(a, b):
    return lax.dot_general(a, b, (((1,), (0,)), ((), ())), preferred_element_type=F32)


def nt(a, b):
    return lax.dot_general(a, b, (((1,), (1,)), ((), ())), preferred_element_type=F32)


def tn(a, b):
    return lax.dot_general(a, b, (((0,), (0,)), ((), ())), preferred_element_type=F32)


def mark(name):
    pass


def rcopy(src, dst, ssem, rsem, device):
    return pltpu.make_async_remote_copy(
        src_ref=src, dst_ref=dst, send_sem=ssem, recv_sem=rsem,
        device_id=device, device_id_type=MESH,
    )


def drain(ref, sem):
    pltpu.make_async_copy(ref, ref, sem).wait()


def time_gain(gains, step_value):
    channels = gains.shape[1]
    place = lax.broadcasted_iota(jnp.int32, (8, channels), 1).astype(F32)
    frequency = jnp.exp(-log_span * place / channels)
    factor = jnp.cos(step_value * frequency)
    return gains * (1.0 + 0.5 * factor[0:1])


def norm_backward(floats, inverse, factor, upstream):
    scaled = upstream * factor
    middle = jnp.mean(floats * scaled, axis=-1, keepdims=True)
    return (inverse * scaled - floats * inverse * inverse * inverse * middle).astype(BF16)


def kernel(
    t_ref, xf_h, dyf_h, xc_h, dyc_h, gf_h, gc_h, wqkv_h, wout_h, cw_h, cwo_h,
    dxf, dxc, gfq, gfo, gcq, gco,
    xf, dyf, xc4, dyc4, gf, gc, wqkv, wout, cw, cwo, xc, ff, fc,
    ag, nrm, kv, edge32, edge, bias, qm, um, kt, vt, nt_all, wall, sall, oexp, odp, otop, osum, odel, att, dqt, dn, gsend, grecv,
    rs_send, rsx, rsz_send, rsz,
    cg, cgb, cgp, c16, c16r, cfin,
    fg, fgb, fgp, fxs, fxr, fzs, fzr, fyr, ffin,
    heard, s_in, s_ag, r_ag, s_h, r_h, s_g, r_g, s_rx, r_rx, s_rz, r_rz,
    s_cc, r_cc, s_c16, r_c16, s_cag, r_cag, s_cf, r_cf,
    s_fc, r_fc, s_fx, r_fx, s_fz, r_fz, s_fy, r_fy, s_fzg, r_fzg, s_fxg, r_fxg, s_ff, r_ff,
):
    b = lax.axis_index("batch")
    gy = lax.axis_index("gy")
    gx = lax.axis_index("gx")
    core = lax.rem(b, 2)
    bz = b // 2
    slot = gx * 4 + gy

    def group(p):
        return (b, lax.rem(p, 4), p // 4)

    def batch(p):
        return (p * 2 + core, gy, gx)

    partner = (b + 1 - 2 * core, gy, gx)

    zlo = b // 16
    yy = lax.rem(bz, 8)
    zz = gy * 2 + zlo

    def along_z(p):
        return (lax.rem(p, 2) * 16 + yy * 2 + core, p // 2, gx)

    def along_x(p):
        return (b, gy, p)

    def along_y(p):
        return (zlo * 16 + p * 2 + core, gy, gx)

    mark("greet")
    loads = [
        pltpu.make_async_copy(h, v, s_in.at[i])
        for i, (h, v) in enumerate((
            (gf_h, gf), (gc_h, gc), (xf_h, xf), (xc_h, xc4), (dyc_h, dyc4), (wqkv_h, wqkv), (wout_h, wout),
            (dyf_h, dyf), (cw_h, cw), (cwo_h, cwo),
        ))
    ]
    for c in loads:
        c.start()
    barrier = pltpu.get_barrier_semaphore()

    def toward(step):
        return (b, lax.rem(gy + step[0] + 4, 4), lax.rem(gx + step[1] + 4, 4))

    near = [toward(FROM[s]) for s in range(1, 9)]
    line = [along_y(lax.rem(yy + 1, 8)), along_y(lax.rem(yy + 7, 8)), (b + 16 - 32 * zlo, gy, gx)]

    def tell(sem, devices):
        for device in devices:
            pl.semaphore_signal(sem, inc=1, device_id=device, device_id_type=MESH)

    tell(barrier, near + line + [partner])

    mark("norms")
    step_value = t_ref[0].astype(F32)
    for c in loads[0:3]:
        c.wait()
    ff[...] = time_gain(gf[...], step_value)
    fc[...] = time_gain(gc[...], step_value)

    xff = xf[...].astype(F32)
    inv_f = lax.rsqrt(jnp.mean(xff * xff, axis=-1, keepdims=True) + eps)
    normf = xff * inv_f * ff[...]
    normed = normf.astype(BF16)
    nrm[0:256, :] = normed
    norm3 = normf.reshape(8, 32, 256)
    for r in range(8):
        edge32[0, 4 * r:4 * r + 4, :] = norm3[r, 0:4, :]
        edge32[1, 4 * r:4 * r + 4, :] = norm3[r, 28:32, :]
    edge[...] = edge32[...].astype(BF16)

    for c in loads[3:5]:
        c.wait()
    for r in range(4):
        xc[4 * r:4 * r + 4, :] = xc4[r].astype(F32)
    xcf = xc[...]
    inv_c = lax.rsqrt(jnp.mean(xcf * xcf, axis=-1, keepdims=True) + eps)
    ag[slot, 0:16, :] = (xcf * inv_c * fc[...]).astype(BF16)
    ag[slot, 16:32, :] = jnp.concatenate([dyc4[r].astype(F32) for r in range(4)], axis=0).astype(BF16)

    mark("barwait")
    pl.semaphore_wait(barrier, 12)

    mark("send0")
    src = {
        LEFT: edge.at[1], RIGHT: edge.at[0],
        TOP: nrm.at[pl.ds(160, 96)], BOTTOM: nrm.at[pl.ds(0, 96)],
        TL: edge.at[1, pl.ds(16, 16)], TR: edge.at[0, pl.ds(16, 16)],
        BL: edge.at[1, pl.ds(0, 16)], BR: edge.at[0, pl.ds(0, 16)],
    }

    def size(s):
        return SEGMENTS[s][1] * SEGMENTS[s][2]

    halo = []
    for s in range(1, 9):
        dy, dx = FROM[s]
        halo.append(rcopy(src[s], nrm.at[pl.ds(SEGMENTS[s][0], size(s))], s_h, r_h,
                          toward((-dy, -dx))))

    up, down, opp = lax.rem(gy + 1, 4), lax.rem(gy + 3, 4), lax.rem(gy + 2, 4)
    right, left, far = lax.rem(gx + 1, 4), lax.rem(gx + 3, 4), lax.rem(gx + 2, 4)
    NEAR, OPP, REST = 0, 2, 3

    def ag_send(g, x, device, arrival, part=None):
        sl = x * 4 + g
        block = ag.at[sl] if part is None else ag.at[sl, pl.ds(16 * part, 16)]
        rcopy(block, block, s_ag, r_ag.at[arrival], device).start()

    for i, g in enumerate((up, down)):
        ag_send(gy, gx, (b, g, gx), NEAR + i)
    for x in (right, left):
        ag_send(gy, gx, (b, gy, x), REST)

    for s in (TL, TR, BL, BR, TOP, BOTTOM, LEFT, RIGHT):
        halo[s - 1].start()
    tell(heard.at[0], near + line)
    mark("qmask")
    for c in loads[5:8]:
        c.wait()
    kv[0:256, :] = nn(normed, wqkv[:, 256:768]).astype(BF16)
    q = nn(normed, wqkv[:, 0:256])
    upst = nt(dyf[...], wout[...])
    lane = lax.broadcasted_iota(jnp.int32, (256, 256), 1) // HD
    for h in range(H_F):
        qm[h * 256:(h + 1) * 256, :] = jnp.where(lane == h, q, 0.0).astype(BF16)
        um[h * 256:(h + 1) * 256, :] = jnp.where(lane == h, upst, 0.0).astype(BF16)
    ok_side = {OWN: None, LEFT: gx > 0, RIGHT: gx < 3, TOP: gy > 0, BOTTOM: gy < 3,
               TL: (gx > 0) & (gy > 0), TR: (gx < 3) & (gy > 0),
               BL: (gx > 0) & (gy < 3), BR: (gx < 3) & (gy < 3)}
    for s, (first, rows, cols, row0, col0) in enumerate(SEGMENTS):
        n = rows * cols
        key = lax.broadcasted_iota(jnp.int32, (n, 256), 0)
        query = lax.broadcasted_iota(jnp.int32, (n, 256), 1)
        dr = key // cols + row0 - query // 32
        dc = lax.rem(key, cols) + col0 - lax.rem(query, 32)
        ok = (dr >= -RAD) & (dr <= RAD) & (dc >= -RAD) & (dc <= RAD)
        floor = jnp.where(ok, 0.0, -1e30).astype(F32)
        if ok_side[s] is not None:
            floor = jnp.minimum(floor, jnp.where(ok_side[s], 0.0, -1e30).astype(F32))
        bias[first:first + n, :] = floor

    mark("own")
    kt[:, 0:256] = kv[0:256, 0:256].T
    vt[:, 0:256] = kv[0:256, 256:512].T
    nt_all[:, 0:256] = nrm[0:256, :].T
    for h in range(H_F):
        heads = slice(h * 256, (h + 1) * 256)
        s = nt(kv[0:256, 0:256], qm[heads, :]) * scale + bias[0:256, :]
        top = jnp.max(s, axis=0, keepdims=True)
        e = jnp.exp(s - top)
        dp = nt(kv[0:256, 256:512], um[heads, :])
        oexp[:, heads] = e
        odp[:, heads] = dp
        otop[h:h + 1, :] = top
        osum[h:h + 1, :] = jnp.sum(e, axis=0, keepdims=True)
        odel[h:h + 1, :] = jnp.sum(e * dp, axis=0, keepdims=True)

    mark("heard0")
    pl.semaphore_wait(heard.at[0], 11)
    tell(heard.at[1], line)
    ag_send(gy, gx, (b, gy, far), REST)
    mark("forward")
    for i, (g, device) in enumerate(((down, (b, up, gx)), (up, (b, down, gx)))):
        drain(ag.at[0], r_ag.at[NEAR + i])
        ag_send(g, gx, device, OPP, i)
        for x in (far, right, left):
            ag_send(g, gx, (b, gy, x), REST)

    mark("halowait")
    drain(nrm.at[pl.ds(256, HALO)], r_h)

    mark("transp")
    pl.semaphore_wait(heard.at[1], 3)
    tell(heard.at[2], line)
    kv[256:KEYS, :] = nn(nrm[256:KEYS, :], wqkv[:, 256:768]).astype(BF16)
    kt[:, 256:KEYS] = kv[256:KEYS, 0:256].T
    vt[:, 256:KEYS] = kv[256:KEYS, 256:512].T
    nt_all[:, 256:KEYS] = nrm[256:KEYS, :].T

    def head(h):
        rows = slice(h * 64, (h + 1) * 64)
        heads = slice(h * 256, (h + 1) * 256)
        s = nt(kv[256:KEYS, 0:256], qm[heads, :]) * scale + bias[256:KEYS, :]
        own_top = otop[h:h + 1, :]
        top = jnp.maximum(own_top, jnp.max(s, axis=0, keepdims=True))
        e = jnp.exp(s - top)
        shrink = jnp.exp(own_top - top)
        inv = 1.0 / (osum[h:h + 1, :] * shrink + jnp.sum(e, axis=0, keepdims=True))
        own_p = oexp[:, heads] * (shrink * inv)
        p = e * inv
        wall[0:256, heads] = own_p.astype(BF16)
        wall[256:KEYS, heads] = p.astype(BF16)
        dp = nt(kv[256:KEYS, 256:512], um[heads, :])
        delta = odel[h:h + 1, :] * (shrink * inv) + jnp.sum(p * dp, axis=0, keepdims=True)
        sall[0:256, heads] = (own_p * (odp[:, heads] - delta)).astype(BF16)
        sall[256:KEYS, heads] = (p * (dp - delta)).astype(BF16)
        att[rows, :] = nn(vt[rows, :], wall[:, heads]).astype(BF16)
        dqt[rows, :] = nn(kt[rows, :], sall[:, heads]) * scale

    mark("head01")
    head(0)
    head(1)
    mark("head23")
    pl.semaphore_wait(heard.at[2], 3)
    tell(heard.at[3], line)
    head(2)
    head(3)

    mark("forward2")
    pl.semaphore_wait(heard.at[3], 3)
    drain(ag.at[0], r_ag.at[OPP])
    for x in (far, right, left):
        ag_send(opp, gx, (b, gy, x), REST)
    mark("finegrad")
    dq = dqt[...].T.astype(BF16)
    dk = (nn(sall[...], qm[...]) * scale).astype(BF16)
    dv = nn(wall[...], um[...]).astype(BF16)
    parts = (
        (nn(nt_all[:, 0:256], dq), nn(nt_all[...], dk)),
        (nn(nt_all[...], dv), nn(att[...], dyf[...])),
    )
    for half in range(2):
        for i in range(2):
            fg[half, :, 256 * i:256 * (i + 1)] = parts[half][i]
            fgb[half, :, 256 * i:256 * (i + 1)] = parts[half][i].astype(BF16)
    fcc = rcopy(fgb.at[1 - core], fgp, s_fc, r_fc, partner)
    fcc.start()

    mark("gsend")
    gsend[...] = (nt(dk[256:KEYS], wqkv[:, 256:512]) + nt(dv[256:KEYS], wqkv[:, 512:768])).astype(BF16)
    for s in range(1, 9):
        dy, dx = FROM[s]
        o = BACK[s]
        c = rcopy(gsend.at[pl.ds(SEGMENTS[s][0] - 256, size(s))],
                  grecv.at[pl.ds(SEGMENTS[o][0] - 256, size(o))],
                  s_g, r_g, toward((dy, dx)))
        c.start()
    dn[...] = (
        nt(dq, wqkv[:, 0:256]) + nt(dk[0:256], wqkv[:, 256:512]) + nt(dv[0:256], wqkv[:, 512:768])
    ).reshape(8, 32, 256)

    def spread(source, dest, ssem, rsem, me, device, each, n=16):
        def body(i, carry):
            p = lax.rem(me + i, n)
            rcopy(source.at[p] if each else source, dest.at[me], ssem, rsem, device(p)).start()
            return carry
        lax.fori_loop(1, n, body, 0)

    def collect(dest, ssem, rsem, n=16):
        drain(dest.at[pl.ds(0, n - 1)], rsem)
        drain(dest.at[pl.ds(0, n - 1)], ssem)

    def total(dest, n=16):
        acc = dest[0].astype(F32)
        for i in range(1, n):
            acc = acc + dest[i].astype(F32)
        return acc

    mark("fccwait")
    fcc.wait_recv()
    fxs[...] = (fg[core] + fgp[...].astype(F32)).astype(BF16).reshape(4, 64, 512)
    spread(fxs, fxr, s_fx, r_fx, gx, along_x, True, n=4)

    mark("agwait")
    drain(ag.at[pl.ds(0, 12)], r_ag.at[REST])
    for c in loads[8:10]:
        c.wait()
    mark("coarse")
    nall = ag[:, 0:16, :].reshape(256, D_C)
    call = ag[:, 16:32, :].reshape(256, D_C)
    proj = nt(cw[...], nall).astype(BF16)
    cqt, ckt, cvt = proj[0:64], proj[64:128], proj[128:192]
    cut = nt(cwo[...], call).astype(BF16)
    cs = tn(ckt, cqt) * scale
    ce = jnp.exp(cs - jnp.max(cs, axis=0, keepdims=True))
    cp = ce * (1.0 / jnp.sum(ce, axis=0, keepdims=True))
    cwt = cp.astype(BF16)
    cot = nn(cvt, cwt).astype(BF16)
    cdp = tn(cvt, cut)
    cdelta = jnp.sum(cp * cdp, axis=0, keepdims=True)
    cslope = (cp * (cdp - cdelta)).astype(BF16)
    cdt = jnp.concatenate(
        [nn(ckt, cslope) * scale, nt(cqt, cslope) * scale, nt(cut, cwt)], axis=0
    ).astype(BF16)
    mark("rs")
    rs_send[...] = tn(cdt, cw[...]).astype(BF16).reshape(4, 4, 16, D_C)
    spread(rs_send, rsx, s_rx, r_rx, gx, along_x, True, n=4)
    mark("cgrad")
    cgq = nn(cdt, nall)
    cgo = nn(cot, call)
    for half in range(2):
        lanes = slice(half * 512, (half + 1) * 512)
        cg[half, 0:192, :] = cgq[:, lanes]
        cg[half, 192:256, :] = cgo[:, lanes]
        cgb[half, 0:192, :] = cgq[:, lanes].astype(BF16)
        cgb[half, 192:256, :] = cgo[:, lanes].astype(BF16)
    cc = rcopy(cgb.at[1 - core], cgp, s_cc, r_cc, partner)
    cc.start()

    mark("fxwait")
    collect(fxr, s_fx, r_fx, 4)
    fxr[gx] = fxs[gx]
    acc = total(fxr, 4)
    for j in range(2):
        fzs[4 * j:4 * j + 4] = acc[:, 256 * j:256 * (j + 1)].astype(BF16).reshape(4, 16, 256)
    fzr[zz] = fzs[zz]
    spread(fzs, fzr, s_fz, r_fz, zz, along_z, True, n=8)
    mark("ccwait")
    cc.wait_recv()
    c16[...] = (cg[core] + cgp[...].astype(F32)).astype(BF16).reshape(16, 16, 512)
    c16r[bz] = c16[bz]
    spread(c16, c16r, s_c16, r_c16, bz, batch, True)

    mark("fzwait")
    collect(fzr, s_fz, r_fz, 8)
    fyr[yy] = total(fzr, 8).astype(BF16)
    spread(fyr.at[yy], fyr, s_fy, r_fy, yy, along_y, False, n=8)

    mark("rsx")
    collect(rsx, s_rx, r_rx, 4)
    rsx[gx] = rs_send[gx]
    rsz_send[...] = total(rsx, 4).astype(BF16)
    spread(rsz_send, rsz, s_rz, r_rz, gy, lambda p: (b, p, gx), True, n=4)

    mark("ghalowait")
    drain(grecv, r_g)

    def owed(s):
        first, rows, cols = SEGMENTS[s][:3]
        return grecv[first - 256:first - 256 + rows * cols, :].astype(F32).reshape(rows, cols, 256)

    mark("dxf")
    dn[0:3, :, :] += owed(TOP)
    dn[5:8, :, :] += owed(BOTTOM)
    for s, row0, col0 in ((LEFT, 0, 0), (RIGHT, 0, 28), (TL, 0, 0), (TR, 0, 28), (BL, 4, 0), (BR, 4, 28)):
        share = owed(s)
        for r in range(SEGMENTS[s][1]):
            dn[row0 + r, col0:col0 + 4, :] += share[r]
    xff = xf[...].astype(F32)
    inv_f = lax.rsqrt(jnp.mean(xff * xff, axis=-1, keepdims=True) + eps)
    dxf[...] = norm_backward(xff, inv_f, ff[...], dn[...].reshape(256, 256))

    mark("c16wait")
    collect(c16r, s_c16, r_c16)
    cmine = cfin.at[core, bz]
    cmine[...] = total(c16r).astype(BF16)
    spread(cmine, cfin.at[core], s_cag, r_cag.at[bz // 4], bz, batch, False)

    mark("fywait")
    collect(fyr, s_fy, r_fy, 8)
    fcol = ffin.at[core, gx]
    fmine = fcol.at[zz]
    fmine[...] = total(fyr, 8).astype(BF16)
    spread(fmine, fcol, s_fzg, r_fzg, zz, along_z, False, n=8)

    mark("rszwait")
    collect(rsz, s_rz, r_rz, 4)
    rsz[gy] = rsz_send[gy]
    dnc = total(rsz, 4)
    xcf = xc[...]
    inv_c = lax.rsqrt(jnp.mean(xcf * xcf, axis=-1, keepdims=True) + eps)
    dxcv = norm_backward(xcf, inv_c, fc[...], dnc)
    for r in range(4):
        dxc[r] = dxcv[4 * r:4 * r + 4]

    mark("fzgwait")
    collect(fcol, s_fzg, r_fzg, 8)

    for i in (1, 3, 2):
        rcopy(fcol, fcol, s_fxg, r_fxg.at[i], (b, gy, lax.rem(gx + i, 4))).start()
    rcopy(fcol, fcol, s_ff, r_ff, partner).start()

    mark("cagwait")
    for k in (1, 2, 3, 4):
        four = lax.rem(bz // 4 + k, 4)
        drain(cfin.at[core, pl.ds(0, 4 if k < 4 else 3)], r_cag.at[four])
        blocks = cfin.at[core, pl.ds(4 * four, 4)]
        rcopy(blocks, blocks, s_cf, r_cf, partner).start()
    mark("fxgwait")
    for i in (1, 3, 2):
        drain(fcol, r_fxg.at[i])
        came = ffin.at[core, lax.rem(gx - i + 4, 4)]
        rcopy(came, came, s_ff, r_ff, partner).start()
    mark("cfwait")
    drain(cfin.at[0], r_cf)
    drain(cfin.at[0], s_cf)
    drain(cfin.at[0, pl.ds(0, 15)], s_cag)
    for half in range(2):
        lanes = slice(half * 512, (half + 1) * 512)
        done = cfin[half].reshape(256, 512)
        gcq[:, lanes] = done[0:192]
        gco[:, lanes] = done[192:256]

    mark("ffwait")
    drain(ffin.at[0], r_ff)
    drain(ffin.at[0], s_ff)
    drain(ffin.at[0, pl.ds(0, 3)], s_fxg)
    for x in range(4):
        rows = slice(64 * x, 64 * (x + 1))
        quarter = [ffin[half, x, 4 * j:4 * j + 4].reshape(64, 256) for half in range(2) for j in range(2)]
        for i in range(3):
            gfq[rows, 256 * i:256 * (i + 1)] = quarter[i]
        gfo[rows, :] = quarter[3]

    mark("sendwait")
    drain(nrm.at[pl.ds(256, HALO)], s_h)
    drain(grecv, s_g)
    drain(ag.at[pl.ds(0, 15)], s_ag)
    cc.wait_send()
    fcc.wait_send()
    mark(None)


def writer(*refs):
    sems = refs[12]
    copies = [pltpu.make_async_copy(refs[i], refs[6 + i], sems.at[i]) for i in range(6)]
    for c in copies:
        c.start()
    for c in copies:
        c.wait()


def local(x_fine, dy_fine, x_coarse, dy_coarse, timestep, fine_gain, coarse_gain,
          fine_qkv, fine_out, coarse_qkv, coarse_out):
    vm = pl.BlockSpec(memory_space=pltpu.VMEM)
    hbm = pl.BlockSpec(memory_space=pltpu.HBM)
    dma = pltpu.SemaphoreType.DMA
    V = pltpu.VMEM
    outs = (
        jax.ShapeDtypeStruct((256, 256), BF16),
        jax.ShapeDtypeStruct((4, 4, D_C), BF16),
        jax.ShapeDtypeStruct((256, 768), BF16),
        jax.ShapeDtypeStruct((256, 256), BF16),
        jax.ShapeDtypeStruct((192, D_C), BF16),
        jax.ShapeDtypeStruct((64, D_C), BF16),
    )
    scratch = [
        V((256, 256), BF16), V((256, 256), BF16), V((4, 4, D_C), BF16), V((4, 4, D_C), BF16),
        V((1, 256), F32), V((1, D_C), F32), V((256, 768), BF16), V((256, 256), BF16),
        V((192, D_C), BF16), V((64, D_C), BF16), V((16, D_C), F32), V((1, 256), F32), V((1, D_C), F32),
        V((16, 32, D_C), BF16), V((KEYS, 256), BF16), V((KEYS, 512), BF16), V((2, 32, 256), F32), V((2, 32, 256), BF16),
        V((KEYS, 256), F32), V((1024, 256), BF16), V((1024, 256), BF16),
        V((256, KEYS), BF16), V((256, KEYS), BF16), V((256, KEYS), BF16),
        V((KEYS, 1024), BF16), V((KEYS, 1024), BF16),
        V((256, 1024), F32), V((256, 1024), F32), V((8, 256), F32), V((8, 256), F32), V((8, 256), F32),
        V((256, 256), BF16), V((256, 256), F32), V((8, 32, 256), F32),
        V((HALO, 256), BF16), V((HALO, 256), BF16),
        V((4, 4, 16, D_C), BF16), V((4, 4, 16, D_C), BF16), V((4, 16, D_C), BF16), V((4, 16, D_C), BF16),
        V((2, 256, 512), F32), V((2, 256, 512), BF16), V((256, 512), BF16),
        V((16, 16, 512), BF16), V((16, 16, 512), BF16), V((2, 16, 16, 512), BF16),
        V((2, 256, 512), F32), V((2, 256, 512), BF16), V((256, 512), BF16),
        V((4, 64, 512), BF16), V((4, 64, 512), BF16), V((8, 16, 256), BF16), V((8, 16, 256), BF16),
        V((8, 16, 256), BF16), V((2, 4, 8, 16, 256), BF16),
        pltpu.SemaphoreType.REGULAR((4,)), dma((10,)), dma, dma((4,)), dma, dma, dma, dma, dma, dma, dma, dma,
        dma, dma, dma, dma, dma, dma((4,)), dma, dma,
        dma, dma, dma, dma, dma, dma, dma, dma, dma, dma, dma, dma((4,)), dma, dma,
    ]
    results = pl.pallas_call(
        kernel,
        out_shape=outs,
        in_specs=[pl.BlockSpec(memory_space=pltpu.SMEM)] + [hbm] * 10,
        out_specs=[vm] * 6,
        scratch_shapes=scratch,
        compiler_params=pltpu.CompilerParams(
            collective_id=0, has_side_effects=True, vmem_limit_bytes=50 * 1024 * 1024
        ),
    )(timestep, *[
        pltpu.with_memory_space_constraint(a, pltpu.HBM) for a in (
            x_fine.reshape(256, D_F), dy_fine.reshape(256, D_F),
            x_coarse.reshape(4, 4, D_C), dy_coarse.reshape(4, 4, D_C),
            fine_gain[None], coarse_gain[None],
            fine_qkv, fine_out, coarse_qkv.reshape(192, D_C), coarse_out,
        )
    ])
    dxf, dxc, gfq, gfo, gcq, gco = pl.pallas_call(
        writer,
        out_shape=tuple(pltpu.HBM(o.shape, o.dtype) for o in outs),
        in_specs=[vm] * 6,
        out_specs=[hbm] * 6,
        scratch_shapes=[dma((6,))],
    )(*[pltpu.with_memory_space_constraint(r, pltpu.VMEM) for r in results])
    return (
        dxf.reshape(x_fine.shape),
        dxc.reshape(x_coarse.shape),
        gfq,
        gfo,
        gcq.reshape(coarse_qkv.shape),
        gco,
    )


def solution(mesh):
    tile = P("batch", "gy", "gx", None)
    heads = P(None, ("gy", "gx"), None)
    rows = P(("gy", "gx"), None)
    return jax.shard_map(
        local,
        mesh=mesh,
        in_specs=(tile, tile, tile, tile, P("batch"), P(), P(), P(), P(), heads, rows),
        out_specs=(tile, tile, P(), P(), heads, rows),
        check_vma=False,
    )
```

```python
import math

import jax
import jax.numpy as jnp
from jax import lax
from jax.experimental import pallas as pl
from jax.experimental.pallas import tpu as pltpu
from jax.sharding import PartitionSpec as P

D_F = 256
H_F = 4
D_C = 1024
HD = 64
RAD = 3
F32 = jnp.float32
BF16 = jnp.bfloat16
MESH = pl.DeviceIdType.MESH

eps = 1e-06
log_span = math.log(1000.0)
scale = 1.0 / math.sqrt(HD)

OWN, LEFT, RIGHT, TOP, BOTTOM, TL, TR, BL, BR = range(9)
SEGMENTS = (
    (0, 8, 32, 0, 0),
    (256, 8, 4, 0, -4),
    (288, 8, 4, 0, 32),
    (320, 3, 32, -3, 0),
    (416, 3, 32, 8, 0),
    (512, 4, 4, -4, -4),
    (528, 4, 4, -4, 32),
    (544, 4, 4, 8, -4),
    (560, 4, 4, 8, 32),
)
KEYS = 576
HALO = KEYS - 256
FROM = {LEFT: (0, -1), RIGHT: (0, 1), TOP: (-1, 0), BOTTOM: (1, 0),
        TL: (-1, -1), TR: (-1, 1), BL: (1, -1), BR: (1, 1)}
BACK = {LEFT: RIGHT, RIGHT: LEFT, TOP: BOTTOM, BOTTOM: TOP, TL: BR, BR: TL, TR: BL, BL: TR}


def nn(a, b):
    return lax.dot_general(a, b, (((1,), (0,)), ((), ())), preferred_element_type=F32)


def nt(a, b):
    return lax.dot_general(a, b, (((1,), (1,)), ((), ())), preferred_element_type=F32)


def tn(a, b):
    return lax.dot_general(a, b, (((0,), (0,)), ((), ())), preferred_element_type=F32)


def mark(name):
    pass


def rcopy(src, dst, ssem, rsem, device):
    return pltpu.make_async_remote_copy(
        src_ref=src, dst_ref=dst, send_sem=ssem, recv_sem=rsem,
        device_id=device, device_id_type=MESH,
    )


def drain(ref, sem):
    pltpu.make_async_copy(ref, ref, sem).wait()


def time_gain(gains, step_value):
    channels = gains.shape[1]
    place = lax.broadcasted_iota(jnp.int32, (8, channels), 1).astype(F32)
    frequency = jnp.exp(-log_span * place / channels)
    factor = jnp.cos(step_value * frequency)
    return gains * (1.0 + 0.5 * factor[0:1])


def norm_backward(floats, inverse, factor, upstream):
    scaled = upstream * factor
    middle = jnp.mean(floats * scaled, axis=-1, keepdims=True)
    return (inverse * scaled - floats * inverse * inverse * inverse * middle).astype(BF16)


def kernel(
    t_ref, xf_h, dyf_h, xc_h, dyc_h, gf_h, gc_h, wqkv_h, wout_h, cw_h, cwo_h,
    dxf, dxc, gfq, gfo, gcq, gco,
    xf, dyf, xc4, dyc4, gf, gc, wqkv, wout, cw, cwo, xc, ff, fc,
    ag, nrm, kv, edge32, edge, bias, qm, um, kt, vt, nt_all, wall, sall, oexp, odp, otop, osum, odel, att, dqt, dn, gsend, grecv,
    rs_send, rsx, rsz_send, rsz,
    cg, cgb, cgp, c16, c16r, cfin,
    fg, fgb, fgp, fxs, fxr, fzs, fzr, fyr, ffin,
    heard, s_in, s_ag, r_ag, s_h, r_h, s_g, r_g, s_rx, r_rx, s_rz, r_rz,
    s_cc, r_cc, s_c16, r_c16, s_cag, r_cag, s_cf, r_cf,
    s_fc, r_fc, s_fx, r_fx, s_fz, r_fz, s_fy, r_fy, s_fzg, r_fzg, s_fxg, r_fxg, s_ff, r_ff,
):
    b = lax.axis_index("batch")
    gy = lax.axis_index("gy")
    gx = lax.axis_index("gx")
    core = lax.rem(b, 2)
    bz = b // 2
    slot = gx * 4 + gy

    def group(p):
        return (b, lax.rem(p, 4), p // 4)

    def batch(p):
        return (p * 2 + core, gy, gx)

    partner = (b + 1 - 2 * core, gy, gx)

    zlo = b // 16
    yy = lax.rem(bz, 8)
    zz = gy * 2 + zlo

    def along_z(p):
        return (lax.rem(p, 2) * 16 + yy * 2 + core, p // 2, gx)

    def along_x(p):
        return (b, gy, p)

    def along_y(p):
        return (zlo * 16 + p * 2 + core, gy, gx)

    mark("greet")
    loads = [
        pltpu.make_async_copy(h, v, s_in.at[i])
        for i, (h, v) in enumerate((
            (gf_h, gf), (gc_h, gc), (xf_h, xf), (xc_h, xc4), (dyc_h, dyc4), (wqkv_h, wqkv), (wout_h, wout),
            (dyf_h, dyf), (cw_h, cw), (cwo_h, cwo),
        ))
    ]
    for c in loads:
        c.start()
    barrier = pltpu.get_barrier_semaphore()

    def toward(step):
        return (b, lax.rem(gy + step[0] + 4, 4), lax.rem(gx + step[1] + 4, 4))

    near = [toward(FROM[s]) for s in range(1, 9)]
    line = [along_y(lax.rem(yy + 1, 8)), along_y(lax.rem(yy + 7, 8)), (b + 16 - 32 * zlo, gy, gx)]

    def tell(sem, devices):
        for device in devices:
            pl.semaphore_signal(sem, inc=1, device_id=device, device_id_type=MESH)

    tell(barrier, near + line + [partner])

    mark("norms")
    step_value = t_ref[0].astype(F32)
    for c in loads[0:3]:
        c.wait()
    ff[...] = time_gain(gf[...], step_value)
    fc[...] = time_gain(gc[...], step_value)

    xff = xf[...].astype(F32)
    inv_f = lax.rsqrt(jnp.mean(xff * xff, axis=-1, keepdims=True) + eps)
    normf = xff * inv_f * ff[...]
    normed = normf.astype(BF16)
    nrm[0:256, :] = normed
    norm3 = normf.reshape(8, 32, 256)
    for r in range(8):
        edge32[0, 4 * r:4 * r + 4, :] = norm3[r, 0:4, :]
        edge32[1, 4 * r:4 * r + 4, :] = norm3[r, 28:32, :]
    edge[...] = edge32[...].astype(BF16)

    for c in loads[3:5]:
        c.wait()
    for r in range(4):
        xc[4 * r:4 * r + 4, :] = xc4[r].astype(F32)
    xcf = xc[...]
    inv_c = lax.rsqrt(jnp.mean(xcf * xcf, axis=-1, keepdims=True) + eps)
    ag[slot, 0:16, :] = (xcf * inv_c * fc[...]).astype(BF16)
    ag[slot, 16:32, :] = jnp.concatenate([dyc4[r].astype(F32) for r in range(4)], axis=0).astype(BF16)

    mark("barwait")
    pl.semaphore_wait(barrier, 12)

    mark("send0")
    src = {
        LEFT: edge.at[1], RIGHT: edge.at[0],
        TOP: nrm.at[pl.ds(160, 96)], BOTTOM: nrm.at[pl.ds(0, 96)],
        TL: edge.at[1, pl.ds(16, 16)], TR: edge.at[0, pl.ds(16, 16)],
        BL: edge.at[1, pl.ds(0, 16)], BR: edge.at[0, pl.ds(0, 16)],
    }

    def size(s):
        return SEGMENTS[s][1] * SEGMENTS[s][2]

    halo = []
    for s in range(1, 9):
        dy, dx = FROM[s]
        halo.append(rcopy(src[s], nrm.at[pl.ds(SEGMENTS[s][0], size(s))], s_h, r_h,
                          toward((-dy, -dx))))

    up, down, opp = lax.rem(gy + 1, 4), lax.rem(gy + 3, 4), lax.rem(gy + 2, 4)
    right, left, far = lax.rem(gx + 1, 4), lax.rem(gx + 3, 4), lax.rem(gx + 2, 4)
    NEAR, OPP, REST = 0, 2, 3

    def ag_send(g, x, device, arrival, part=None):
        sl = x * 4 + g
        block = ag.at[sl] if part is None else ag.at[sl, pl.ds(16 * part, 16)]
        rcopy(block, block, s_ag, r_ag.at[arrival], device).start()

    for i, g in enumerate((up, down)):
        ag_send(gy, gx, (b, g, gx), NEAR + i)
    for x in (right, left):
        ag_send(gy, gx, (b, gy, x), REST)

    for s in (TL, TR, BL, BR, TOP, BOTTOM, LEFT, RIGHT):
        halo[s - 1].start()
    tell(heard.at[0], near + line)
    mark("qmask")
    for c in loads[5:8]:
        c.wait()
    kv[0:256, :] = nn(normed, wqkv[:, 256:768]).astype(BF16)
    q = nn(normed, wqkv[:, 0:256])
    upst = nt(dyf[...], wout[...])
    lane = lax.broadcasted_iota(jnp.int32, (256, 256), 1) // HD
    for h in range(H_F):
        qm[h * 256:(h + 1) * 256, :] = jnp.where(lane == h, q, 0.0).astype(BF16)
        um[h * 256:(h + 1) * 256, :] = jnp.where(lane == h, upst, 0.0).astype(BF16)
    ok_side = {OWN: None, LEFT: gx > 0, RIGHT: gx < 3, TOP: gy > 0, BOTTOM: gy < 3,
               TL: (gx > 0) & (gy > 0), TR: (gx < 3) & (gy > 0),
               BL: (gx > 0) & (gy < 3), BR: (gx < 3) & (gy < 3)}
    for s, (first, rows, cols, row0, col0) in enumerate(SEGMENTS):
        n = rows * cols
        key = lax.broadcasted_iota(jnp.int32, (n, 256), 0)
        query = lax.broadcasted_iota(jnp.int32, (n, 256), 1)
        dr = key // cols + row0 - query // 32
        dc = lax.rem(key, cols) + col0 - lax.rem(query, 32)
        ok = (dr >= -RAD) & (dr <= RAD) & (dc >= -RAD) & (dc <= RAD)
        floor = jnp.where(ok, 0.0, -1e30).astype(F32)
        if ok_side[s] is not None:
            floor = jnp.minimum(floor, jnp.where(ok_side[s], 0.0, -1e30).astype(F32))
        bias[first:first + n, :] = floor

    mark("own")
    kt[:, 0:256] = kv[0:256, 0:256].T
    vt[:, 0:256] = kv[0:256, 256:512].T
    nt_all[:, 0:256] = nrm[0:256, :].T
    for h in range(H_F):
        heads = slice(h * 256, (h + 1) * 256)
        s = nt(kv[0:256, 0:256], qm[heads, :]) * scale + bias[0:256, :]
        top = jnp.max(s, axis=0, keepdims=True)
        e = jnp.exp(s - top)
        dp = nt(kv[0:256, 256:512], um[heads, :])
        oexp[:, heads] = e
        odp[:, heads] = dp
        otop[h:h + 1, :] = top
        osum[h:h + 1, :] = jnp.sum(e, axis=0, keepdims=True)
        odel[h:h + 1, :] = jnp.sum(e * dp, axis=0, keepdims=True)

    mark("heard0")
    pl.semaphore_wait(heard.at[0], 11)
    tell(heard.at[1], line)
    ag_send(gy, gx, (b, gy, far), REST)
    mark("forward")
    for i, (g, device) in enumerate(((down, (b, up, gx)), (up, (b, down, gx)))):
        drain(ag.at[0], r_ag.at[NEAR + i])
        ag_send(g, gx, device, OPP, i)
        for x in (far, right, left):
            ag_send(g, gx, (b, gy, x), REST)

    mark("halowait")
    drain(nrm.at[pl.ds(256, HALO)], r_h)

    mark("transp")
    pl.semaphore_wait(heard.at[1], 3)
    tell(heard.at[2], line)
    kv[256:KEYS, :] = nn(nrm[256:KEYS, :], wqkv[:, 256:768]).astype(BF16)
    kt[:, 256:KEYS] = kv[256:KEYS, 0:256].T
    vt[:, 256:KEYS] = kv[256:KEYS, 256:512].T
    nt_all[:, 256:KEYS] = nrm[256:KEYS, :].T

    def head(h):
        rows = slice(h * 64, (h + 1) * 64)
        heads = slice(h * 256, (h + 1) * 256)
        s = nt(kv[256:KEYS, 0:256], qm[heads, :]) * scale + bias[256:KEYS, :]
        own_top = otop[h:h + 1, :]
        top = jnp.maximum(own_top, jnp.max(s, axis=0, keepdims=True))
        e = jnp.exp(s - top)
        shrink = jnp.exp(own_top - top)
        inv = 1.0 / (osum[h:h + 1, :] * shrink + jnp.sum(e, axis=0, keepdims=True))
        own_p = oexp[:, heads] * (shrink * inv)
        p = e * inv
        wall[0:256, heads] = own_p.astype(BF16)
        wall[256:KEYS, heads] = p.astype(BF16)
        dp = nt(kv[256:KEYS, 256:512], um[heads, :])
        delta = odel[h:h + 1, :] * (shrink * inv) + jnp.sum(p * dp, axis=0, keepdims=True)
        sall[0:256, heads] = (own_p * (odp[:, heads] - delta)).astype(BF16)
        sall[256:KEYS, heads] = (p * (dp - delta)).astype(BF16)
        att[rows, :] = nn(vt[rows, :], wall[:, heads]).astype(BF16)
        dqt[rows, :] = nn(kt[rows, :], sall[:, heads]) * scale

    mark("head01")
    head(0)
    head(1)
    mark("head23")
    pl.semaphore_wait(heard.at[2], 3)
    tell(heard.at[3], line)
    head(2)
    head(3)

    mark("forward2")
    pl.semaphore_wait(heard.at[3], 3)
    drain(ag.at[0], r_ag.at[OPP])
    for x in (far, right, left):
        ag_send(opp, gx, (b, gy, x), REST)
    mark("finegrad")
    dq = dqt[...].T.astype(BF16)
    dk = (nn(sall[...], qm[...]) * scale).astype(BF16)
    dv = nn(wall[...], um[...]).astype(BF16)
    parts = (
        (nn(nt_all[:, 0:256], dq), nn(nt_all[...], dk)),
        (nn(nt_all[...], dv), nn(att[...], dyf[...])),
    )
    for half in range(2):
        for i in range(2):
            fg[half, :, 256 * i:256 * (i + 1)] = parts[half][i]
            fgb[half, :, 256 * i:256 * (i + 1)] = parts[half][i].astype(BF16)
    fcc = rcopy(fgb.at[1 - core], fgp, s_fc, r_fc, partner)
    fcc.start()

    mark("gsend")
    gsend[...] = (nt(dk[256:KEYS], wqkv[:, 256:512]) + nt(dv[256:KEYS], wqkv[:, 512:768])).astype(BF16)
    for s in range(1, 9):
        dy, dx = FROM[s]
        o = BACK[s]
        c = rcopy(gsend.at[pl.ds(SEGMENTS[s][0] - 256, size(s))],
                  grecv.at[pl.ds(SEGMENTS[o][0] - 256, size(o))],
                  s_g, r_g, toward((dy, dx)))
        c.start()
    dn[...] = (
        nt(dq, wqkv[:, 0:256]) + nt(dk[0:256], wqkv[:, 256:512]) + nt(dv[0:256], wqkv[:, 512:768])
    ).reshape(8, 32, 256)

    def spread(source, dest, ssem, rsem, me, device, each, n=16):
        ring = min(n, 8)
        for other in range(n // ring - 1, -1, -1):
            for o in sorted(range(ring), key=lambda o: -min(o, ring - o)):
                if (other, o) == (0, 0):
                    continue
                p = lax.rem(me + o, ring) if n == ring else lax.rem(me // 8 + other, 2) * 8 + lax.rem(me + o, 8)
                rcopy(source.at[p] if each else source, dest.at[me], ssem, rsem, device(p)).start()

    def collect(dest, ssem, rsem, n=16):
        drain(dest.at[pl.ds(0, n - 1)], rsem)
        drain(dest.at[pl.ds(0, n - 1)], ssem)

    def total(dest, n=16):
        acc = dest[0].astype(F32)
        for i in range(1, n):
            acc = acc + dest[i].astype(F32)
        return acc

    mark("fccwait")
    fcc.wait_recv()
    fxs[...] = (fg[core] + fgp[...].astype(F32)).astype(BF16).reshape(4, 64, 512)
    spread(fxs, fxr, s_fx, r_fx, gx, along_x, True, n=4)

    mark("agwait")
    drain(ag.at[pl.ds(0, 12)], r_ag.at[REST])
    for c in loads[8:10]:
        c.wait()
    mark("coarse")
    nall = ag[:, 0:16, :].reshape(256, D_C)
    call = ag[:, 16:32, :].reshape(256, D_C)
    proj = nt(cw[...], nall).astype(BF16)
    cqt, ckt, cvt = proj[0:64], proj[64:128], proj[128:192]
    cut = nt(cwo[...], call).astype(BF16)
    cs = tn(ckt, cqt) * scale
    ce = jnp.exp(cs - jnp.max(cs, axis=0, keepdims=True))
    cp = ce * (1.0 / jnp.sum(ce, axis=0, keepdims=True))
    cwt = cp.astype(BF16)
    cot = nn(cvt, cwt).astype(BF16)
    cdp = tn(cvt, cut)
    cdelta = jnp.sum(cp * cdp, axis=0, keepdims=True)
    cslope = (cp * (cdp - cdelta)).astype(BF16)
    cdt = jnp.concatenate(
        [nn(ckt, cslope) * scale, nt(cqt, cslope) * scale, nt(cut, cwt)], axis=0
    ).astype(BF16)
    mark("rs")
    rs_send[...] = tn(cdt, cw[...]).astype(BF16).reshape(4, 4, 16, D_C)
    spread(rs_send, rsx, s_rx, r_rx, gx, along_x, True, n=4)
    mark("cgrad")
    cgq = nn(cdt, nall)
    cgo = nn(cot, call)
    for half in range(2):
        lanes = slice(half * 512, (half + 1) * 512)
        cg[half, 0:192, :] = cgq[:, lanes]
        cg[half, 192:256, :] = cgo[:, lanes]
        cgb[half, 0:192, :] = cgq[:, lanes].astype(BF16)
        cgb[half, 192:256, :] = cgo[:, lanes].astype(BF16)
    cc = rcopy(cgb.at[1 - core], cgp, s_cc, r_cc, partner)
    cc.start()

    mark("fxwait")
    collect(fxr, s_fx, r_fx, 4)
    fxr[gx] = fxs[gx]
    acc = total(fxr, 4)
    for j in range(2):
        fzs[4 * j:4 * j + 4] = acc[:, 256 * j:256 * (j + 1)].astype(BF16).reshape(4, 16, 256)
    fzr[zz] = fzs[zz]
    spread(fzs, fzr, s_fz, r_fz, zz, along_z, True, n=8)
    mark("ccwait")
    cc.wait_recv()
    c16[...] = (cg[core] + cgp[...].astype(F32)).astype(BF16).reshape(16, 16, 512)
    c16r[bz] = c16[bz]
    spread(c16, c16r, s_c16, r_c16, bz, batch, True)

    mark("fzwait")
    collect(fzr, s_fz, r_fz, 8)
    fyr[yy] = total(fzr, 8).astype(BF16)
    spread(fyr.at[yy], fyr, s_fy, r_fy, yy, along_y, False, n=8)

    mark("rsx")
    collect(rsx, s_rx, r_rx, 4)
    rsx[gx] = rs_send[gx]
    rsz_send[...] = total(rsx, 4).astype(BF16)
    spread(rsz_send, rsz, s_rz, r_rz, gy, lambda p: (b, p, gx), True, n=4)

    mark("ghalowait")
    drain(grecv, r_g)

    def owed(s):
        first, rows, cols = SEGMENTS[s][:3]
        return grecv[first - 256:first - 256 + rows * cols, :].astype(F32).reshape(rows, cols, 256)

    mark("dxf")
    dn[0:3, :, :] += owed(TOP)
    dn[5:8, :, :] += owed(BOTTOM)
    for s, row0, col0 in ((LEFT, 0, 0), (RIGHT, 0, 28), (TL, 0, 0), (TR, 0, 28), (BL, 4, 0), (BR, 4, 28)):
        share = owed(s)
        for r in range(SEGMENTS[s][1]):
            dn[row0 + r, col0:col0 + 4, :] += share[r]
    xff = xf[...].astype(F32)
    inv_f = lax.rsqrt(jnp.mean(xff * xff, axis=-1, keepdims=True) + eps)
    dxf[...] = norm_backward(xff, inv_f, ff[...], dn[...].reshape(256, 256))

    mark("fywait")
    collect(fyr, s_fy, r_fy, 8)
    fcol = ffin.at[core, gx]
    fmine = fcol.at[zz]
    fmine[...] = total(fyr, 8).astype(BF16)
    spread(fmine, fcol, s_fzg, r_fzg, zz, along_z, False, n=8)

    mark("c16wait")
    collect(c16r, s_c16, r_c16)
    cmine = cfin.at[core, bz]
    cmine[...] = total(c16r).astype(BF16)
    spread(cmine, cfin.at[core], s_cag, r_cag.at[bz // 4], bz, batch, False)

    mark("rszwait")
    collect(rsz, s_rz, r_rz, 4)
    rsz[gy] = rsz_send[gy]
    dnc = total(rsz, 4)
    xcf = xc[...]
    inv_c = lax.rsqrt(jnp.mean(xcf * xcf, axis=-1, keepdims=True) + eps)
    dxcv = norm_backward(xcf, inv_c, fc[...], dnc)
    for r in range(4):
        dxc[r] = dxcv[4 * r:4 * r + 4]

    mark("fzgwait")
    collect(fcol, s_fzg, r_fzg, 8)

    for i in (1, 3, 2):
        rcopy(fcol, fcol, s_fxg, r_fxg.at[i], (b, gy, lax.rem(gx + i, 4))).start()
    rcopy(fcol, fcol, s_ff, r_ff, partner).start()

    mark("cagwait")
    for k in (1, 2, 3, 4):
        four = lax.rem(bz // 4 + k, 4)
        drain(cfin.at[core, pl.ds(0, 4 if k < 4 else 3)], r_cag.at[four])
        blocks = cfin.at[core, pl.ds(4 * four, 4)]
        rcopy(blocks, blocks, s_cf, r_cf, partner).start()
    mark("fxgwait")
    for i in (1, 3, 2):
        drain(fcol, r_fxg.at[i])
        came = ffin.at[core, lax.rem(gx - i + 4, 4)]
        rcopy(came, came, s_ff, r_ff, partner).start()
    mark("cfwait")
    drain(cfin.at[0], r_cf)
    drain(cfin.at[0], s_cf)
    drain(cfin.at[0, pl.ds(0, 15)], s_cag)
    for half in range(2):
        lanes = slice(half * 512, (half + 1) * 512)
        done = cfin[half].reshape(256, 512)
        gcq[:, lanes] = done[0:192]
        gco[:, lanes] = done[192:256]

    mark("ffwait")
    drain(ffin.at[0], r_ff)
    drain(ffin.at[0], s_ff)
    drain(ffin.at[0, pl.ds(0, 3)], s_fxg)
    for x in range(4):
        rows = slice(64 * x, 64 * (x + 1))
        quarter = [ffin[half, x, 4 * j:4 * j + 4].reshape(64, 256) for half in range(2) for j in range(2)]
        for i in range(3):
            gfq[rows, 256 * i:256 * (i + 1)] = quarter[i]
        gfo[rows, :] = quarter[3]

    mark("sendwait")
    drain(nrm.at[pl.ds(256, HALO)], s_h)
    drain(grecv, s_g)
    drain(ag.at[pl.ds(0, 15)], s_ag)
    cc.wait_send()
    fcc.wait_send()
    mark(None)


def writer(*refs):
    sems = refs[12]
    copies = [pltpu.make_async_copy(refs[i], refs[6 + i], sems.at[i]) for i in range(6)]
    for c in copies:
        c.start()
    for c in copies:
        c.wait()


def local(x_fine, dy_fine, x_coarse, dy_coarse, timestep, fine_gain, coarse_gain,
          fine_qkv, fine_out, coarse_qkv, coarse_out):
    vm = pl.BlockSpec(memory_space=pltpu.VMEM)
    hbm = pl.BlockSpec(memory_space=pltpu.HBM)
    dma = pltpu.SemaphoreType.DMA
    V = pltpu.VMEM
    outs = (
        jax.ShapeDtypeStruct((256, 256), BF16),
        jax.ShapeDtypeStruct((4, 4, D_C), BF16),
        jax.ShapeDtypeStruct((256, 768), BF16),
        jax.ShapeDtypeStruct((256, 256), BF16),
        jax.ShapeDtypeStruct((192, D_C), BF16),
        jax.ShapeDtypeStruct((64, D_C), BF16),
    )
    scratch = [
        V((256, 256), BF16), V((256, 256), BF16), V((4, 4, D_C), BF16), V((4, 4, D_C), BF16),
        V((1, 256), F32), V((1, D_C), F32), V((256, 768), BF16), V((256, 256), BF16),
        V((192, D_C), BF16), V((64, D_C), BF16), V((16, D_C), F32), V((1, 256), F32), V((1, D_C), F32),
        V((16, 32, D_C), BF16), V((KEYS, 256), BF16), V((KEYS, 512), BF16), V((2, 32, 256), F32), V((2, 32, 256), BF16),
        V((KEYS, 256), F32), V((1024, 256), BF16), V((1024, 256), BF16),
        V((256, KEYS), BF16), V((256, KEYS), BF16), V((256, KEYS), BF16),
        V((KEYS, 1024), BF16), V((KEYS, 1024), BF16),
        V((256, 1024), F32), V((256, 1024), F32), V((8, 256), F32), V((8, 256), F32), V((8, 256), F32),
        V((256, 256), BF16), V((256, 256), F32), V((8, 32, 256), F32),
        V((HALO, 256), BF16), V((HALO, 256), BF16),
        V((4, 4, 16, D_C), BF16), V((4, 4, 16, D_C), BF16), V((4, 16, D_C), BF16), V((4, 16, D_C), BF16),
        V((2, 256, 512), F32), V((2, 256, 512), BF16), V((256, 512), BF16),
        V((16, 16, 512), BF16), V((16, 16, 512), BF16), V((2, 16, 16, 512), BF16),
        V((2, 256, 512), F32), V((2, 256, 512), BF16), V((256, 512), BF16),
        V((4, 64, 512), BF16), V((4, 64, 512), BF16), V((8, 16, 256), BF16), V((8, 16, 256), BF16),
        V((8, 16, 256), BF16), V((2, 4, 8, 16, 256), BF16),
        pltpu.SemaphoreType.REGULAR((4,)), dma((10,)), dma, dma((4,)), dma, dma, dma, dma, dma, dma, dma, dma,
        dma, dma, dma, dma, dma, dma((4,)), dma, dma,
        dma, dma, dma, dma, dma, dma, dma, dma, dma, dma, dma, dma((4,)), dma, dma,
    ]
    results = pl.pallas_call(
        kernel,
        out_shape=outs,
        in_specs=[pl.BlockSpec(memory_space=pltpu.SMEM)] + [hbm] * 10,
        out_specs=[vm] * 6,
        scratch_shapes=scratch,
        compiler_params=pltpu.CompilerParams(
            collective_id=0, has_side_effects=True, vmem_limit_bytes=50 * 1024 * 1024
        ),
    )(timestep, *[
        pltpu.with_memory_space_constraint(a, pltpu.HBM) for a in (
            x_fine.reshape(256, D_F), dy_fine.reshape(256, D_F),
            x_coarse.reshape(4, 4, D_C), dy_coarse.reshape(4, 4, D_C),
            fine_gain[None], coarse_gain[None],
            fine_qkv, fine_out, coarse_qkv.reshape(192, D_C), coarse_out,
        )
    ])
    dxf, dxc, gfq, gfo, gcq, gco = pl.pallas_call(
        writer,
        out_shape=tuple(pltpu.HBM(o.shape, o.dtype) for o in outs),
        in_specs=[vm] * 6,
        out_specs=[hbm] * 6,
        scratch_shapes=[dma((6,))],
    )(*[pltpu.with_memory_space_constraint(r, pltpu.VMEM) for r in results])
    return (
        dxf.reshape(x_fine.shape),
        dxc.reshape(x_coarse.shape),
        gfq,
        gfo,
        gcq.reshape(coarse_qkv.shape),
        gco,
    )


def solution(mesh):
    tile = P("batch", "gy", "gx", None)
    heads = P(None, ("gy", "gx"), None)
    rows = P(("gy", "gx"), None)
    return jax.shard_map(
        local,
        mesh=mesh,
        in_specs=(tile, tile, tile, tile, P("batch"), P(), P(), P(), P(), heads, rows),
        out_specs=(tile, tile, P(), P(), heads, rows),
        check_vma=False,
    )
```

```python
import math

import jax
import jax.numpy as jnp
from jax import lax
from jax.experimental import pallas as pl
from jax.experimental.pallas import tpu as pltpu
from jax.sharding import PartitionSpec as P

D_F = 256
H_F = 4
D_C = 1024
HD = 64
RAD = 3
F32 = jnp.float32
BF16 = jnp.bfloat16
MESH = pl.DeviceIdType.MESH

eps = 1e-06
log_span = math.log(1000.0)
scale = 1.0 / math.sqrt(HD)

OWN, LEFT, RIGHT, TOP, BOTTOM, TL, TR, BL, BR = range(9)
SEGMENTS = (
    (0, 8, 32, 0, 0),
    (256, 8, 4, 0, -4),
    (288, 8, 4, 0, 32),
    (320, 3, 32, -3, 0),
    (416, 3, 32, 8, 0),
    (512, 4, 4, -4, -4),
    (528, 4, 4, -4, 32),
    (544, 4, 4, 8, -4),
    (560, 4, 4, 8, 32),
)
KEYS = 576
HALO = KEYS - 256
FROM = {LEFT: (0, -1), RIGHT: (0, 1), TOP: (-1, 0), BOTTOM: (1, 0),
        TL: (-1, -1), TR: (-1, 1), BL: (1, -1), BR: (1, 1)}
BACK = {LEFT: RIGHT, RIGHT: LEFT, TOP: BOTTOM, BOTTOM: TOP, TL: BR, BR: TL, TR: BL, BL: TR}


def nn(a, b):
    return lax.dot_general(a, b, (((1,), (0,)), ((), ())), preferred_element_type=F32)


def nt(a, b):
    return lax.dot_general(a, b, (((1,), (1,)), ((), ())), preferred_element_type=F32)


def tn(a, b):
    return lax.dot_general(a, b, (((0,), (0,)), ((), ())), preferred_element_type=F32)


def mark(name):
    pass


def rcopy(src, dst, ssem, rsem, device):
    return pltpu.make_async_remote_copy(
        src_ref=src, dst_ref=dst, send_sem=ssem, recv_sem=rsem,
        device_id=device, device_id_type=MESH,
    )


def drain(ref, sem):
    pltpu.make_async_copy(ref, ref, sem).wait()


def time_wave(channels, step_value):
    place = lax.broadcasted_iota(jnp.int32, (8, channels), 1).astype(F32)
    frequency = jnp.exp(-log_span * place / channels)
    factor = jnp.cos(step_value * frequency)
    return 1.0 + 0.5 * factor[0:1]


def norm_backward(floats, inverse, factor, upstream):
    scaled = upstream * factor
    middle = jnp.mean(floats * scaled, axis=-1, keepdims=True)
    return (inverse * scaled - floats * inverse * inverse * inverse * middle).astype(BF16)


def kernel(
    t_ref, xf_h, dyf_h, xc_h, dyc_h, gf_h, gc_h, wqkv_h, wout_h, cw_h, cwo_h,
    dxf, dxc, gfq, gfo, gcq, gco,
    xf, dyf, xc4, dyc4, gf, gc, wqkv, wout, cw, cwo, xc, ff, fc,
    ag, nrm, kv, edge32, edge, bias, qm, um, kt, vt, nt_all, wall, sall, oexp, odp, otop, osum, odel, att, dqt, dn, gsend, grecv,
    rs_send, rsx, rsz_send, rsz,
    cg, cgb, cgp, c16, c16r, cfin,
    fg, fgb, fgp, fxs, fxr, fzs, fzr, fyr, ffin,
    heard, s_in, s_ag, r_ag, s_h, r_h, s_g, r_g, s_rx, r_rx, s_rz, r_rz,
    s_cc, r_cc, s_c16, r_c16, s_cag, r_cag, s_cf, r_cf,
    s_fc, r_fc, s_fx, r_fx, s_fz, r_fz, s_fy, r_fy, s_fzg, r_fzg, s_fxg, r_fxg, s_ff, r_ff,
):
    b = lax.axis_index("batch")
    gy = lax.axis_index("gy")
    gx = lax.axis_index("gx")
    core = lax.rem(b, 2)
    bz = b // 2
    slot = gx * 4 + gy

    def group(p):
        return (b, lax.rem(p, 4), p // 4)

    def batch(p):
        return (p * 2 + core, gy, gx)

    partner = (b + 1 - 2 * core, gy, gx)

    zlo = b // 16
    yy = lax.rem(bz, 8)
    zz = gy * 2 + zlo

    def along_z(p):
        return (lax.rem(p, 2) * 16 + yy * 2 + core, p // 2, gx)

    def along_x(p):
        return (b, gy, p)

    def along_y(p):
        return (zlo * 16 + p * 2 + core, gy, gx)

    mark("greet")
    loads = [
        pltpu.make_async_copy(h, v, s_in.at[i])
        for i, (h, v) in enumerate((
            (gf_h, gf), (gc_h, gc), (xf_h, xf), (xc_h, xc4), (dyc_h, dyc4), (wqkv_h, wqkv), (wout_h, wout),
            (dyf_h, dyf), (cw_h, cw), (cwo_h, cwo),
        ))
    ]
    for c in loads:
        c.start()
    barrier = pltpu.get_barrier_semaphore()

    def toward(step):
        return (b, lax.rem(gy + step[0] + 4, 4), lax.rem(gx + step[1] + 4, 4))

    near = [toward(FROM[s]) for s in range(1, 9)]
    line = [along_y(lax.rem(yy + 1, 8)), along_y(lax.rem(yy + 7, 8)), (b + 16 - 32 * zlo, gy, gx)]

    def tell(sem, devices):
        for device in devices:
            pl.semaphore_signal(sem, inc=1, device_id=device, device_id_type=MESH)

    tell(barrier, near + line + [partner])

    mark("norms")
    step_value = t_ref[0].astype(F32)
    ff[...] = time_wave(D_F, step_value)
    fc[...] = time_wave(D_C, step_value)
    for c in loads[0:3]:
        c.wait()
    ff[...] = gf[...] * ff[...]
    fc[...] = gc[...] * fc[...]

    xff = xf[...].astype(F32)
    inv_f = lax.rsqrt(jnp.mean(xff * xff, axis=-1, keepdims=True) + eps)
    normf = xff * inv_f * ff[...]
    normed = normf.astype(BF16)
    nrm[0:256, :] = normed
    norm3 = normf.reshape(8, 32, 256)
    for r in range(8):
        edge32[0, 4 * r:4 * r + 4, :] = norm3[r, 0:4, :]
        edge32[1, 4 * r:4 * r + 4, :] = norm3[r, 28:32, :]
    edge[...] = edge32[...].astype(BF16)

    for c in loads[3:5]:
        c.wait()
    for r in range(4):
        xc[4 * r:4 * r + 4, :] = xc4[r].astype(F32)
    xcf = xc[...]
    inv_c = lax.rsqrt(jnp.mean(xcf * xcf, axis=-1, keepdims=True) + eps)
    ag[slot, 0:16, :] = (xcf * inv_c * fc[...]).astype(BF16)
    ag[slot, 16:32, :] = jnp.concatenate([dyc4[r].astype(F32) for r in range(4)], axis=0).astype(BF16)

    mark("barwait")
    pl.semaphore_wait(barrier, 12)

    mark("send0")
    src = {
        LEFT: edge.at[1], RIGHT: edge.at[0],
        TOP: nrm.at[pl.ds(160, 96)], BOTTOM: nrm.at[pl.ds(0, 96)],
        TL: edge.at[1, pl.ds(16, 16)], TR: edge.at[0, pl.ds(16, 16)],
        BL: edge.at[1, pl.ds(0, 16)], BR: edge.at[0, pl.ds(0, 16)],
    }

    def size(s):
        return SEGMENTS[s][1] * SEGMENTS[s][2]

    halo = []
    for s in range(1, 9):
        dy, dx = FROM[s]
        halo.append(rcopy(src[s], nrm.at[pl.ds(SEGMENTS[s][0], size(s))], s_h, r_h,
                          toward((-dy, -dx))))

    up, down, opp = lax.rem(gy + 1, 4), lax.rem(gy + 3, 4), lax.rem(gy + 2, 4)
    right, left, far = lax.rem(gx + 1, 4), lax.rem(gx + 3, 4), lax.rem(gx + 2, 4)
    NEAR, OPP, REST = 0, 2, 3

    def ag_send(g, x, device, arrival, part=None):
        sl = x * 4 + g
        block = ag.at[sl] if part is None else ag.at[sl, pl.ds(16 * part, 16)]
        rcopy(block, block, s_ag, r_ag.at[arrival], device).start()

    for i, g in enumerate((up, down)):
        ag_send(gy, gx, (b, g, gx), NEAR + i)
    for x in (right, left):
        ag_send(gy, gx, (b, gy, x), REST)

    for s in (TL, TR, BL, BR, TOP, BOTTOM, LEFT, RIGHT):
        halo[s - 1].start()
    tell(heard.at[0], near + line)
    mark("qmask")
    for c in loads[5:8]:
        c.wait()
    kv[0:256, :] = nn(normed, wqkv[:, 256:768]).astype(BF16)
    q = nn(normed, wqkv[:, 0:256])
    upst = nt(dyf[...], wout[...])
    lane = lax.broadcasted_iota(jnp.int32, (256, 256), 1) // HD
    for h in range(H_F):
        qm[h * 256:(h + 1) * 256, :] = jnp.where(lane == h, q, 0.0).astype(BF16)
        um[h * 256:(h + 1) * 256, :] = jnp.where(lane == h, upst, 0.0).astype(BF16)
    ok_side = {OWN: None, LEFT: gx > 0, RIGHT: gx < 3, TOP: gy > 0, BOTTOM: gy < 3,
               TL: (gx > 0) & (gy > 0), TR: (gx < 3) & (gy > 0),
               BL: (gx > 0) & (gy < 3), BR: (gx < 3) & (gy < 3)}
    for s, (first, rows, cols, row0, col0) in enumerate(SEGMENTS):
        n = rows * cols
        key = lax.broadcasted_iota(jnp.int32, (n, 256), 0)
        query = lax.broadcasted_iota(jnp.int32, (n, 256), 1)
        dr = key // cols + row0 - query // 32
        dc = lax.rem(key, cols) + col0 - lax.rem(query, 32)
        ok = (dr >= -RAD) & (dr <= RAD) & (dc >= -RAD) & (dc <= RAD)
        floor = jnp.where(ok, 0.0, -1e30).astype(F32)
        if ok_side[s] is not None:
            floor = jnp.minimum(floor, jnp.where(ok_side[s], 0.0, -1e30).astype(F32))
        bias[first:first + n, :] = floor

    mark("own")
    kt[:, 0:256] = kv[0:256, 0:256].T
    vt[:, 0:256] = kv[0:256, 256:512].T
    nt_all[:, 0:256] = nrm[0:256, :].T
    for h in range(H_F):
        heads = slice(h * 256, (h + 1) * 256)
        s = nt(kv[0:256, 0:256], qm[heads, :]) * scale + bias[0:256, :]
        top = jnp.max(s, axis=0, keepdims=True)
        e = jnp.exp(s - top)
        dp = nt(kv[0:256, 256:512], um[heads, :])
        oexp[:, heads] = e
        odp[:, heads] = dp
        otop[h:h + 1, :] = top
        osum[h:h + 1, :] = jnp.sum(e, axis=0, keepdims=True)
        odel[h:h + 1, :] = jnp.sum(e * dp, axis=0, keepdims=True)

    mark("heard0")
    pl.semaphore_wait(heard.at[0], 11)
    tell(heard.at[1], line)
    ag_send(gy, gx, (b, gy, far), REST)
    mark("forward")
    for i, (g, device) in enumerate(((down, (b, up, gx)), (up, (b, down, gx)))):
        drain(ag.at[0], r_ag.at[NEAR + i])
        ag_send(g, gx, device, OPP, i)
        for x in (far, right, left):
            ag_send(g, gx, (b, gy, x), REST)

    mark("halowait")
    drain(nrm.at[pl.ds(256, HALO)], r_h)

    mark("transp")
    pl.semaphore_wait(heard.at[1], 3)
    tell(heard.at[2], line)
    kv[256:KEYS, :] = nn(nrm[256:KEYS, :], wqkv[:, 256:768]).astype(BF16)
    kt[:, 256:KEYS] = kv[256:KEYS, 0:256].T
    vt[:, 256:KEYS] = kv[256:KEYS, 256:512].T
    nt_all[:, 256:KEYS] = nrm[256:KEYS, :].T

    def head(h):
        rows = slice(h * 64, (h + 1) * 64)
        heads = slice(h * 256, (h + 1) * 256)
        s = nt(kv[256:KEYS, 0:256], qm[heads, :]) * scale + bias[256:KEYS, :]
        own_top = otop[h:h + 1, :]
        top = jnp.maximum(own_top, jnp.max(s, axis=0, keepdims=True))
        e = jnp.exp(s - top)
        shrink = jnp.exp(own_top - top)
        inv = 1.0 / (osum[h:h + 1, :] * shrink + jnp.sum(e, axis=0, keepdims=True))
        own_p = oexp[:, heads] * (shrink * inv)
        p = e * inv
        wall[0:256, heads] = own_p.astype(BF16)
        wall[256:KEYS, heads] = p.astype(BF16)
        dp = nt(kv[256:KEYS, 256:512], um[heads, :])
        delta = odel[h:h + 1, :] * (shrink * inv) + jnp.sum(p * dp, axis=0, keepdims=True)
        sall[0:256, heads] = (own_p * (odp[:, heads] - delta)).astype(BF16)
        sall[256:KEYS, heads] = (p * (dp - delta)).astype(BF16)
        att[rows, :] = nn(vt[rows, :], wall[:, heads]).astype(BF16)
        dqt[rows, :] = nn(kt[rows, :], sall[:, heads]) * scale

    mark("head01")
    head(0)
    head(1)
    mark("head23")
    head(2)
    head(3)

    mark("forward2")
    drain(ag.at[0], r_ag.at[OPP])
    for x in (far, right, left):
        ag_send(opp, gx, (b, gy, x), REST)
    mark("finegrad")
    dq = dqt[...].T.astype(BF16)
    dk = (nn(sall[...], qm[...]) * scale).astype(BF16)
    dv = nn(wall[...], um[...]).astype(BF16)
    parts = (
        (nn(nt_all[:, 0:256], dq), nn(nt_all[...], dk)),
        (nn(nt_all[...], dv), nn(att[...], dyf[...])),
    )
    for half in range(2):
        for i in range(2):
            fg[half, :, 256 * i:256 * (i + 1)] = parts[half][i]
            fgb[half, :, 256 * i:256 * (i + 1)] = parts[half][i].astype(BF16)
    fcc = rcopy(fgb.at[1 - core], fgp, s_fc, r_fc, partner)
    fcc.start()

    mark("gsend")
    gsend[...] = (nt(dk[256:KEYS], wqkv[:, 256:512]) + nt(dv[256:KEYS], wqkv[:, 512:768])).astype(BF16)
    for s in range(1, 9):
        dy, dx = FROM[s]
        o = BACK[s]
        c = rcopy(gsend.at[pl.ds(SEGMENTS[s][0] - 256, size(s))],
                  grecv.at[pl.ds(SEGMENTS[o][0] - 256, size(o))],
                  s_g, r_g, toward((dy, dx)))
        c.start()
    dn[...] = (
        nt(dq, wqkv[:, 0:256]) + nt(dk[0:256], wqkv[:, 256:512]) + nt(dv[0:256], wqkv[:, 512:768])
    ).reshape(8, 32, 256)

    def spread(source, dest, ssem, rsem, me, device, each, n=16):
        ring = min(n, 8)
        for other in range(n // ring - 1, -1, -1):
            for o in sorted(range(ring), key=lambda o: -min(o, ring - o)):
                if (other, o) == (0, 0):
                    continue
                p = lax.rem(me + o, ring) if n == ring else lax.rem(me // 8 + other, 2) * 8 + lax.rem(me + o, 8)
                rcopy(source.at[p] if each else source, dest.at[me], ssem, rsem, device(p)).start()

    def collect(dest, ssem, rsem, n=16):
        drain(dest.at[pl.ds(0, n - 1)], rsem)
        drain(dest.at[pl.ds(0, n - 1)], ssem)

    def total(dest, n=16):
        acc = dest[0].astype(F32)
        for i in range(1, n):
            acc = acc + dest[i].astype(F32)
        return acc

    mark("fccwait")
    fcc.wait_recv()
    fxs[...] = (fg[core] + fgp[...].astype(F32)).astype(BF16).reshape(4, 64, 512)
    spread(fxs, fxr, s_fx, r_fx, gx, along_x, True, n=4)

    pl.semaphore_wait(heard.at[2], 3)
    tell(heard.at[3], line)
    mark("agwait")
    drain(ag.at[pl.ds(0, 12)], r_ag.at[REST])
    for c in loads[8:10]:
        c.wait()
    mark("coarse")
    nall = ag[:, 0:16, :].reshape(256, D_C)
    call = ag[:, 16:32, :].reshape(256, D_C)
    proj = nt(cw[...], nall).astype(BF16)
    cqt, ckt, cvt = proj[0:64], proj[64:128], proj[128:192]
    cut = nt(cwo[...], call).astype(BF16)
    cs = tn(ckt, cqt) * scale
    ce = jnp.exp(cs - jnp.max(cs, axis=0, keepdims=True))
    cp = ce * (1.0 / jnp.sum(ce, axis=0, keepdims=True))
    cwt = cp.astype(BF16)
    cot = nn(cvt, cwt).astype(BF16)
    cdp = tn(cvt, cut)
    cdelta = jnp.sum(cp * cdp, axis=0, keepdims=True)
    cslope = (cp * (cdp - cdelta)).astype(BF16)
    cdt = jnp.concatenate(
        [nn(ckt, cslope) * scale, nt(cqt, cslope) * scale, nt(cut, cwt)], axis=0
    ).astype(BF16)
    mark("rs")
    rs_send[...] = tn(cdt, cw[...]).astype(BF16).reshape(4, 4, 16, D_C)
    spread(rs_send, rsx, s_rx, r_rx, gx, along_x, True, n=4)
    mark("cgrad")
    cgq = nn(cdt, nall)
    cgo = nn(cot, call)
    for half in range(2):
        lanes = slice(half * 512, (half + 1) * 512)
        cg[half, 0:192, :] = cgq[:, lanes]
        cg[half, 192:256, :] = cgo[:, lanes]
        cgb[half, 0:192, :] = cgq[:, lanes].astype(BF16)
        cgb[half, 192:256, :] = cgo[:, lanes].astype(BF16)
    cc = rcopy(cgb.at[1 - core], cgp, s_cc, r_cc, partner)
    cc.start()

    pl.semaphore_wait(heard.at[3], 3)
    mark("fxwait")
    collect(fxr, s_fx, r_fx, 4)
    fxr[gx] = fxs[gx]
    acc = total(fxr, 4)
    for j in range(2):
        fzs[4 * j:4 * j + 4] = acc[:, 256 * j:256 * (j + 1)].astype(BF16).reshape(4, 16, 256)
    fzr[zz] = fzs[zz]
    spread(fzs, fzr, s_fz, r_fz, zz, along_z, True, n=8)
    mark("ccwait")
    cc.wait_recv()
    c16[...] = (cg[core] + cgp[...].astype(F32)).astype(BF16).reshape(16, 16, 512)
    c16r[bz] = c16[bz]
    spread(c16, c16r, s_c16, r_c16, bz, batch, True)

    mark("fzwait")
    collect(fzr, s_fz, r_fz, 8)
    fyr[yy] = total(fzr, 8).astype(BF16)
    spread(fyr.at[yy], fyr, s_fy, r_fy, yy, along_y, False, n=8)

    mark("rsx")
    collect(rsx, s_rx, r_rx, 4)
    rsx[gx] = rs_send[gx]
    rsz_send[...] = total(rsx, 4).astype(BF16)
    spread(rsz_send, rsz, s_rz, r_rz, gy, lambda p: (b, p, gx), True, n=4)

    mark("ghalowait")
    drain(grecv, r_g)

    def owed(s):
        first, rows, cols = SEGMENTS[s][:3]
        return grecv[first - 256:first - 256 + rows * cols, :].astype(F32).reshape(rows, cols, 256)

    mark("dxf")
    dn[0:3, :, :] += owed(TOP)
    dn[5:8, :, :] += owed(BOTTOM)
    for s, row0, col0 in ((LEFT, 0, 0), (RIGHT, 0, 28), (TL, 0, 0), (TR, 0, 28), (BL, 4, 0), (BR, 4, 28)):
        share = owed(s)
        for r in range(SEGMENTS[s][1]):
            dn[row0 + r, col0:col0 + 4, :] += share[r]
    xff = xf[...].astype(F32)
    inv_f = lax.rsqrt(jnp.mean(xff * xff, axis=-1, keepdims=True) + eps)
    dxf[...] = norm_backward(xff, inv_f, ff[...], dn[...].reshape(256, 256))

    mark("fywait")
    collect(fyr, s_fy, r_fy, 8)
    fcol = ffin.at[core, gx]
    fmine = fcol.at[zz]
    fmine[...] = total(fyr, 8).astype(BF16)
    spread(fmine, fcol, s_fzg, r_fzg, zz, along_z, False, n=8)

    mark("c16wait")
    collect(c16r, s_c16, r_c16)
    cmine = cfin.at[core, bz]
    cmine[...] = total(c16r).astype(BF16)
    spread(cmine, cfin.at[core], s_cag, r_cag.at[bz // 4], bz, batch, False)

    mark("rszwait")
    collect(rsz, s_rz, r_rz, 4)
    rsz[gy] = rsz_send[gy]
    dnc = total(rsz, 4)
    xcf = xc[...]
    inv_c = lax.rsqrt(jnp.mean(xcf * xcf, axis=-1, keepdims=True) + eps)
    dxcv = norm_backward(xcf, inv_c, fc[...], dnc)
    for r in range(4):
        dxc[r] = dxcv[4 * r:4 * r + 4]

    mark("fzgwait")
    collect(fcol, s_fzg, r_fzg, 8)

    for i in (1, 3, 2):
        rcopy(fcol, fcol, s_fxg, r_fxg.at[i], (b, gy, lax.rem(gx + i, 4))).start()
    rcopy(fcol, fcol, s_ff, r_ff, partner).start()

    mark("cagwait")
    for k in (1, 2, 3, 4):
        four = lax.rem(bz // 4 + k, 4)
        drain(cfin.at[core, pl.ds(0, 4 if k < 4 else 3)], r_cag.at[four])
        blocks = cfin.at[core, pl.ds(4 * four, 4)]
        rcopy(blocks, blocks, s_cf, r_cf, partner).start()
    mark("fxgwait")
    for i in (1, 3, 2):
        drain(fcol, r_fxg.at[i])
        came = ffin.at[core, lax.rem(gx - i + 4, 4)]
        rcopy(came, came, s_ff, r_ff, partner).start()
    mark("cfwait")
    drain(cfin.at[0], r_cf)
    drain(cfin.at[0], s_cf)
    drain(cfin.at[0, pl.ds(0, 15)], s_cag)
    for half in range(2):
        lanes = slice(half * 512, (half + 1) * 512)
        done = cfin[half].reshape(256, 512)
        gcq[:, lanes] = done[0:192]
        gco[:, lanes] = done[192:256]

    mark("ffwait")
    drain(ffin.at[0], r_ff)
    drain(ffin.at[0], s_ff)
    drain(ffin.at[0, pl.ds(0, 3)], s_fxg)
    for x in range(4):
        rows = slice(64 * x, 64 * (x + 1))
        quarter = [ffin[half, x, 4 * j:4 * j + 4].reshape(64, 256) for half in range(2) for j in range(2)]
        for i in range(3):
            gfq[rows, 256 * i:256 * (i + 1)] = quarter[i]
        gfo[rows, :] = quarter[3]

    mark("sendwait")
    drain(nrm.at[pl.ds(256, HALO)], s_h)
    drain(grecv, s_g)
    drain(ag.at[pl.ds(0, 15)], s_ag)
    cc.wait_send()
    fcc.wait_send()
    mark(None)


def writer(*refs):
    sems = refs[12]
    copies = [pltpu.make_async_copy(refs[i], refs[6 + i], sems.at[i]) for i in range(6)]
    for c in copies:
        c.start()
    for c in copies:
        c.wait()


def local(x_fine, dy_fine, x_coarse, dy_coarse, timestep, fine_gain, coarse_gain,
          fine_qkv, fine_out, coarse_qkv, coarse_out):
    vm = pl.BlockSpec(memory_space=pltpu.VMEM)
    hbm = pl.BlockSpec(memory_space=pltpu.HBM)
    dma = pltpu.SemaphoreType.DMA
    V = pltpu.VMEM
    outs = (
        jax.ShapeDtypeStruct((256, 256), BF16),
        jax.ShapeDtypeStruct((4, 4, D_C), BF16),
        jax.ShapeDtypeStruct((256, 768), BF16),
        jax.ShapeDtypeStruct((256, 256), BF16),
        jax.ShapeDtypeStruct((192, D_C), BF16),
        jax.ShapeDtypeStruct((64, D_C), BF16),
    )
    scratch = [
        V((256, 256), BF16), V((256, 256), BF16), V((4, 4, D_C), BF16), V((4, 4, D_C), BF16),
        V((1, 256), F32), V((1, D_C), F32), V((256, 768), BF16), V((256, 256), BF16),
        V((192, D_C), BF16), V((64, D_C), BF16), V((16, D_C), F32), V((1, 256), F32), V((1, D_C), F32),
        V((16, 32, D_C), BF16), V((KEYS, 256), BF16), V((KEYS, 512), BF16), V((2, 32, 256), F32), V((2, 32, 256), BF16),
        V((KEYS, 256), F32), V((1024, 256), BF16), V((1024, 256), BF16),
        V((256, KEYS), BF16), V((256, KEYS), BF16), V((256, KEYS), BF16),
        V((KEYS, 1024), BF16), V((KEYS, 1024), BF16),
        V((256, 1024), F32), V((256, 1024), F32), V((8, 256), F32), V((8, 256), F32), V((8, 256), F32),
        V((256, 256), BF16), V((256, 256), F32), V((8, 32, 256), F32),
        V((HALO, 256), BF16), V((HALO, 256), BF16),
        V((4, 4, 16, D_C), BF16), V((4, 4, 16, D_C), BF16), V((4, 16, D_C), BF16), V((4, 16, D_C), BF16),
        V((2, 256, 512), F32), V((2, 256, 512), BF16), V((256, 512), BF16),
        V((16, 16, 512), BF16), V((16, 16, 512), BF16), V((2, 16, 16, 512), BF16),
        V((2, 256, 512), F32), V((2, 256, 512), BF16), V((256, 512), BF16),
        V((4, 64, 512), BF16), V((4, 64, 512), BF16), V((8, 16, 256), BF16), V((8, 16, 256), BF16),
        V((8, 16, 256), BF16), V((2, 4, 8, 16, 256), BF16),
        pltpu.SemaphoreType.REGULAR((4,)), dma((10,)), dma, dma((4,)), dma, dma, dma, dma, dma, dma, dma, dma,
        dma, dma, dma, dma, dma, dma((4,)), dma, dma,
        dma, dma, dma, dma, dma, dma, dma, dma, dma, dma, dma, dma((4,)), dma, dma,
    ]
    results = pl.pallas_call(
        kernel,
        out_shape=outs,
        in_specs=[pl.BlockSpec(memory_space=pltpu.SMEM)] + [hbm] * 10,
        out_specs=[vm] * 6,
        scratch_shapes=scratch,
        compiler_params=pltpu.CompilerParams(
            collective_id=0, has_side_effects=True, vmem_limit_bytes=50 * 1024 * 1024
        ),
    )(timestep, *[
        pltpu.with_memory_space_constraint(a, pltpu.HBM) for a in (
            x_fine.reshape(256, D_F), dy_fine.reshape(256, D_F),
            x_coarse.reshape(4, 4, D_C), dy_coarse.reshape(4, 4, D_C),
            fine_gain[None], coarse_gain[None],
            fine_qkv, fine_out, coarse_qkv.reshape(192, D_C), coarse_out,
        )
    ])
    dxf, dxc, gfq, gfo, gcq, gco = pl.pallas_call(
        writer,
        out_shape=tuple(pltpu.HBM(o.shape, o.dtype) for o in outs),
        in_specs=[vm] * 6,
        out_specs=[hbm] * 6,
        scratch_shapes=[dma((6,))],
    )(*[pltpu.with_memory_space_constraint(r, pltpu.VMEM) for r in results])
    return (
        dxf.reshape(x_fine.shape),
        dxc.reshape(x_coarse.shape),
        gfq,
        gfo,
        gcq.reshape(coarse_qkv.shape),
        gco,
    )


def solution(mesh):
    tile = P("batch", "gy", "gx", None)
    heads = P(None, ("gy", "gx"), None)
    rows = P(("gy", "gx"), None)
    return jax.shard_map(
        local,
        mesh=mesh,
        in_specs=(tile, tile, tile, tile, P("batch"), P(), P(), P(), P(), heads, rows),
        out_specs=(tile, tile, P(), P(), heads, rows),
        check_vma=False,
    )
```
